256 devices in a mesh: tm: 8 (over y, z_lo), chan: 32 (over z_hi, x, core).
Axes of the slice: x: 4, y: 4, z: 8 (z_hi: 4, z_lo: 2; z = z_hi * 2 + z_lo), core: 2. Of those that a mesh axis runs over, the one named last changes fastest.
Arguments:
- recording: float32 [8, 256, 2048], P('tm', 'chan'), may hold values from -22 to 22
- blind_mask: int32 [8, 2048, 256], P('tm', 'chan'), may hold values 0 or 1
- dw_kernels: float32 [3, 32, 9], replicated, may hold values from -2 to 2
- pw_weights: float32 [3, 32, 32], replicated, may hold values from -1 to 1
- biases: float32 [3, 32], replicated, may hold values from -3 to 3
- head_weights: float32 [32], replicated, may hold values from -1 to 1
Outputs:
- dw_grad: float32 [3, 32, 9], replicated
- pw_grad: float32 [3, 32, 32], replicated
- bias_grad: float32 [3, 32], replicated
- head_grad: float32 [32], replicated
- denoised: float32 [8, 256, 2048], P('tm', 'chan')
The draws below stay inside these ranges and needn't reach their ends.
All inputs are finite; a program needn't handle non-finite values. No bound on the sum of `blind_mask` on one device may be relied on, other than what follows from the above.
Results may differ from the reference program's by a relative error of at most 0.0003.
Values sent between devices are 32-bit elements; how exact they have to be, the bound alone decides.
A program may use at most 128 MiB of HBM per device.

```python
import math
import jax
import jax.numpy as jnp
from jax import lax

F = 32
TS = 256
SPOT_EVERY = 8
CH = 2048
WINDOWS = 8


def draw_recording(key, part):
    subkeys = jax.random.split(key, 3)
    column = jnp.arange(CH, dtype=jnp.float32) / max(CH - 1, 1)
    trend = jnp.exp(math.log(3.0) * column)
    roughness = jnp.exp(jax.random.uniform(subkeys[0], (CH,), jnp.float32, 0.0, math.log(10.0 / 3.0)))
    channel_gain = trend * roughness / 3.0
    time_gain = jnp.exp(jax.random.uniform(subkeys[1], (WINDOWS, TS, 1), jnp.float32, math.log(0.6), math.log(1.6)))
    noise_part = jnp.clip(jax.random.normal(subkeys[2], (WINDOWS, TS, CH), jnp.float32), -4.0, 4.0)
    return (noise_part * time_gain * channel_gain[None, None, :]).astype(jnp.float32)


def with_ends(result, own_key, least, high):
    extent = result.shape
    place = [jax.random.randint(jax.random.fold_in(own_key, axis), (), 0, extent[axis]) for axis in range(len(extent))]
    result = result.at[tuple(place)].set(least)
    longest = extent.index(max(extent))
    place[longest] = (place[longest] + 1) % extent[longest]
    return result.at[tuple(place)].set(high)


def bell_draw(stream_key, extent, scale, most, kind=jnp.bfloat16):
    values = scale * jax.random.normal(stream_key, extent, jnp.float32)
    return jnp.clip(values, min=-most, max=most).astype(kind)


def setup_inputs(seed: int = 0) -> dict:
    seeds = jax.random.split(jax.random.key(seed), 7)
    return {
        "recording": draw_recording(jax.random.fold_in(seeds[6], 71), 0),
        "blind_mask": with_ends((jax.random.randint(seeds[1], (WINDOWS, CH, TS), 0, SPOT_EVERY) < 1).astype(jnp.int32), jax.random.fold_in(seeds[1], 1), 0, 1),
        "dw_kernels": bell_draw(seeds[2], (3, F, 9), 9 ** -0.5, 2.0, jnp.float32),
        "pw_weights": bell_draw(seeds[3], (3, F, F), F ** -0.5, 1.0, jnp.float32),
        "biases": bell_draw(seeds[4], (3, F), 0.5, 3.0, jnp.float32),
        "head_weights": bell_draw(seeds[5], (F,), F ** -0.5, 1.0, jnp.float32),
    }


def depthwise(padded, kernel, cols, length):
    total = None
    for tap_row in range(3):
        for tap_col in range(3):
            weight = kernel[:, 3 * tap_row + tap_col][:, None, None]
            term = weight * padded[:, tap_row:tap_row + cols, tap_col:tap_col + length]
            total = term if total is None else total + term
    return total

def window_loss(params, signal, spots):
    dw_kernels, pw_weights, biases, head_weights = params
    current = jnp.where(spots == 1, jnp.zeros_like(signal), signal)[None]
    for layer_index in range(3):
        padded = jnp.pad(current, ((0, 0), (1, 1), (1, 1)))
        spread = depthwise(padded, dw_kernels[layer_index], CH, TS)
        pre = jnp.einsum('gf,fct->gct', pw_weights[layer_index], spread, precision=lax.Precision.HIGHEST)
        pre = pre + biases[layer_index][:, None, None]
        current = jax.nn.silu(pre)
    output = jnp.einsum('f,fct->ct', head_weights, current, precision=lax.Precision.HIGHEST)
    misfit = jnp.where(spots == 1, output - signal, jnp.zeros_like(output))
    loss = jnp.sum(misfit * misfit) * (SPOT_EVERY / (WINDOWS * CH * TS))
    return (loss, output)

def reference(recording, blind_mask, dw_kernels, pw_weights, biases, head_weights):
    params = (dw_kernels, pw_weights, biases, head_weights)
    grad_fn = jax.grad(window_loss, has_aux=True)

    def advance(totals, inputs):
        signal, spots = inputs
        grads, output = grad_fn(params, signal, spots)
        return (jax.tree.map(jnp.add, totals, grads), output)
    zeros = jax.tree.map(jnp.zeros_like, params)
    totals, outputs = lax.scan(advance, zeros, (jnp.swapaxes(recording, 1, 2), blind_mask))
    return (totals[0], totals[1], totals[2], totals[3], jnp.swapaxes(outputs, 1, 2))
```

```python
import functools

import jax
import jax.numpy as jnp
from jax import lax
from jax.experimental import pallas as pl
from jax.experimental.pallas import tpu as pltpu
from jax.sharding import PartitionSpec as P

SPOT_EVERY = 8
F = 32
T = 256
OWN = 64
HALO = 3
OUT = 6
INN = 8
ROWS = OUT * F
COLS = INN * F
NBLK = 11
MESH = pl.DeviceIdType.MESH
F32 = jnp.float32
BF16 = jnp.bfloat16


def iota(shape, dim):
    return lax.broadcasted_iota(jnp.int32, shape, dim)


def split(x):
    hi = x.astype(BF16)
    return hi, (x - hi.astype(F32)).astype(BF16)


def later(x):
    first = iota((x.shape[0], 128), 1) == 0
    a, b = pltpu.roll(x[:, :128], 1, 1), pltpu.roll(x[:, 128:], 1, 1)
    return jnp.concatenate([jnp.where(first, 0.0, a), jnp.where(first, a, b)], axis=1)


def earlier(x):
    last = iota((x.shape[0], 128), 1) == 127
    a, b = pltpu.roll(x[:, :128], 127, 1), pltpu.roll(x[:, 128:], 127, 1)
    return jnp.concatenate([jnp.where(last, b, a), jnp.where(last, 0.0, b)], axis=1)


def dot(a, b):
    return jnp.dot(a, b, preferred_element_type=F32)


def dot_t(a, b):
    return lax.dot_general(a, b, (((1,), (1,)), ((), ())), preferred_element_type=F32)


def as_row(column):
    same = iota((F, COLS), 0) == (iota((F, COLS), 1) & (F - 1))
    return jnp.sum(jnp.where(same, column, 0.0), axis=0, keepdims=True)


def fill_windows(rec_ref, send):
    lane = iota((8, 128), 1)
    tiles = rec_ref.shape[2] // 128
    zero = jnp.zeros((8, 128), F32)
    tile = [rec_ref[0, :, 128 * k : 128 * k + 128] for k in range(tiles)]
    for k in range(tiles):
        before = tile[k - 1] if k > 0 else zero
        after = tile[k + 1] if k < tiles - 1 else zero
        even = jnp.where(lane < HALO, pltpu.roll(before, HALO, 1), pltpu.roll(tile[k], HALO, 1))
        odd = jnp.where(
            lane < OWN + HALO,
            pltpu.roll(tile[k], OWN + HALO, 1),
            pltpu.roll(after, OWN + HALO, 1),
        )
        send[16 * k : 16 * k + 8, :] = even
        send[16 * k + 8 : 16 * k + 16, :] = odd


def comm_in(nchan, rec_ref, mask_ref, win_ref, maskx_ref, send, sems, bsems):
    me = lax.axis_index("chan")
    right, left = lax.rem(me + 1, nchan), lax.rem(me + nchan - 1, nchan)
    barrier = pltpu.get_barrier_semaphore()

    def greet(k, carry):
        pl.semaphore_signal(
            barrier, inc=1, device_id={"chan": lax.rem(me + k, nchan)}, device_id_type=MESH
        )
        return carry

    lax.fori_loop(1, nchan, greet, 0)
    fill_windows(rec_ref, send)
    pl.semaphore_wait(barrier, nchan - 1)

    def tile_copy(peer):
        return pltpu.make_async_remote_copy(
            src_ref=send.at[pl.ds(pl.multiple_of(peer * 8, 8), 8), :],
            dst_ref=win_ref.at[pl.ds(pl.multiple_of(me * 8, 8), 8), :],
            send_sem=sems.at[0],
            recv_sem=sems.at[1],
            device_id={"chan": peer},
            device_id_type=MESH,
        )

    to_right = pltpu.make_async_remote_copy(
        src_ref=mask_ref.at[0, pl.ds(OWN - 8, 8), :],
        dst_ref=maskx_ref.at[pl.ds(0, 8), :],
        send_sem=bsems.at[0],
        recv_sem=bsems.at[1],
        device_id={"chan": right},
        device_id_type=MESH,
    )
    to_left = pltpu.make_async_remote_copy(
        src_ref=mask_ref.at[0, pl.ds(0, 8), :],
        dst_ref=maskx_ref.at[pl.ds(OWN + 8, 8), :],
        send_sem=bsems.at[2],
        recv_sem=bsems.at[3],
        device_id={"chan": left},
        device_id_type=MESH,
    )
    to_right.start()
    to_left.start()

    def push(k, carry):
        tile_copy(lax.rem(me + k, nchan)).start()
        return carry

    lax.fori_loop(1, nchan, push, 0)
    mine = pl.ds(pl.multiple_of(me * 8, 8), 8)
    win_ref[mine, :] = send[mine, :]
    maskx_ref[8 : OWN + 8, :] = mask_ref[0]
    rest = 8 * (nchan - 1)
    every = pltpu.make_async_remote_copy(
        src_ref=send.at[pl.ds(0, rest), :],
        dst_ref=win_ref.at[pl.ds(0, rest), :],
        send_sem=sems.at[0],
        recv_sem=sems.at[1],
        device_id={"chan": right},
        device_id_type=MESH,
    )
    every.wait()
    to_right.wait()
    to_left.wait()


def forward_weights(lhs, pw, dw):
    wide = jnp.concatenate([pw] * INN, axis=1)
    ci = iota((F, COLS), 1) >> 5
    rows = [as_row(dw[:, tap : tap + 1]) for tap in range(9)]
    for j in range(3):
        for co in range(OUT):
            taps = jnp.zeros((F, COLS), F32)
            for i in range(3):
                taps = jnp.where(ci == co + i, rows[3 * i + j], taps)
            hi, lo = split(wide * taps)
            at = slice(j * ROWS + co * F, j * ROWS + co * F + F)
            lhs[at, 0:COLS] = hi
            lhs[at, COLS : 2 * COLS] = lo
            lhs[at, 2 * COLS : 3 * COLS] = hi


def backward_weights(lhs, pw_t, dw):
    wide = jnp.concatenate([pw_t] * INN, axis=1)
    ci = iota((F, COLS), 1) >> 5
    cols = [jnp.broadcast_to(dw[:, tap : tap + 1], (F, COLS)) for tap in range(9)]
    for j in range(3):
        for co in range(OUT):
            taps = jnp.zeros((F, COLS), F32)
            for i in range(3):
                taps = jnp.where(ci == co + 2 - i, cols[3 * i + j], taps)
            hi, lo = split(wide * taps)
            at = slice(j * ROWS + co * F, j * ROWS + co * F + F)
            lhs[at, 0:COLS] = hi
            lhs[at, COLS : 2 * COLS] = lo
            lhs[at, 2 * COLS : 3 * COLS] = hi


def first_weights(lhs, pw, dw):
    lane = iota((F, 144), 1)
    part = (lane >= 48).astype(jnp.int32) + (lane >= 96).astype(jnp.int32)
    spot = lane - 48 * part
    j_of, ci = spot >> 4, spot & 15
    cols = [
        jnp.sum(pw * as_row(dw[:, tap : tap + 1])[:, :F], axis=1, keepdims=True)
        for tap in range(9)
    ]
    for co in range(8):
        taps = jnp.zeros((F, 144), F32)
        for tap in range(9):
            here = (ci == co + tap // 3) & (j_of == tap % 3)
            taps = jnp.where(here, cols[tap], taps)
        hi = taps.astype(BF16).astype(F32)
        lhs[co * F : co * F + F, :] = jnp.where(part == 1, taps - hi, hi).astype(BF16)


def tripled(hi, lo):
    return jnp.concatenate([hi, hi, lo], axis=0)


def silu_parts(pre):
    s = 0.5 * jnp.tanh(0.5 * pre) + 0.5
    a = pre * s
    return a, s + (a - a * s)


def mixed(lhs, hi, lo, flip):
    prod = dot(lhs[...], tripled(hi, lo))
    first, mid, last = prod[:ROWS], prod[ROWS : 2 * ROWS], prod[2 * ROWS :]
    if flip:
        first, last = last, first
    return mid + later(first) + earlier(last)


def fold(x):
    y = x[:, :128] + x[:, 128:]
    y = y + pltpu.roll(y, 64, 1)
    y = y + pltpu.roll(y, 32, 1)
    return y[:, :F]


def shifted_triple(g):
    parts = []
    for x in (earlier(g), g, later(g)):
        hi, lo = split(x)
        parts.append(jnp.concatenate([hi, lo, hi], axis=1))
    return jnp.concatenate(parts, axis=0)


def add_channels(acc, g):
    total = acc[...]
    for k in range(OUT):
        total = total + g[k * F : k * F + F]
    acc[...] = total


def compute(
    nchan, scale, win_ref, maskx_ref, dw_ref, pw_ref, bias_ref, head_ref, out_ref, pack_ref,
    sig, coef, wins, lhs0, lhs_f, lhs_b, a1h, a1l, a2h, a2l, d0, d1,
    g2h, g2l, g1h, g1l, g0h, g0l, acc, acc0, bacc, hacc, bcol, outs,
):
    me = lax.axis_index("chan")
    dw = [dw_ref[l] for l in range(3)]
    pw = [pw_ref[l] for l in range(3)]

    first_weights(lhs0, pw[0], dw[0])
    for l in (1, 2):
        forward_weights(lhs_f.at[l - 1], pw[l], dw[l])
        backward_weights(lhs_b.at[l - 1], pw[l].T, dw[l])
    for l in range(3):
        bcol[l] = jnp.broadcast_to(bias_ref[:, l : l + 1], (F, T))
    bcol[3] = jnp.broadcast_to(head_ref[...], (F, T))

    turned = win_ref[...].T
    sig[...] = turned[:80]
    blind = maskx_ref[5:85, :] == 1
    coef[...] = jnp.where(blind, 2.0 * scale, 0.0)
    act0 = jnp.where(blind, 0.0, turned[:80])
    wins[0] = later(act0)
    wins[1] = act0
    wins[2] = earlier(act0)

    zero2 = jnp.zeros((2 * F, T), BF16)
    for ref in (g2h, g2l, g1h, g1l):
        ref[: 2 * F, :] = zero2
    for ref in (g1h, g1l):
        ref[68 * F :, :] = jnp.zeros((6 * F, T), BF16)
    for ref in (a2h, a2l):
        ref[66 * F :, :] = zero2
    acc[...] = jnp.zeros_like(acc)
    acc0[...] = jnp.zeros_like(acc0)
    bacc[...] = jnp.zeros_like(bacc)
    hacc[...] = jnp.zeros_like(hacc)
    outs[...] = jnp.zeros_like(outs)

    def columns(b):
        return [split(wins[j, pl.ds(pl.multiple_of(8 * b, 8), 16), :]) for j in range(3)]

    def layer0(b, carry):
        parts = columns(b)
        hi = jnp.concatenate([p[0] for p in parts], axis=0)
        lo = jnp.concatenate([p[1] for p in parts], axis=0)
        pre = dot(lhs0[...], tripled(hi, lo))
        pre = pre + jnp.concatenate([bcol[0]] * 8, axis=0)
        a, d = silu_parts(pre)
        at = pl.ds(pl.multiple_of(b * 8 * F, F), 8 * F)
        a1h[at, :], a1l[at, :] = split(a)
        d0[at, :] = d
        return carry

    lax.fori_loop(0, 9, layer0, 0)

    def clear(ends, refs):
        for ref in refs:
            ref[ends, :] = jnp.zeros(((ends.stop - ends.start), T), ref.dtype)

    @pl.when(me == 0)
    def _():
        clear(slice(0, 2 * F), (a1h, a1l, d0))

    @pl.when(me == nchan - 1)
    def _():
        clear(slice(66 * F, 68 * F), (a1h, a1l, d0))

    def inputs(b):
        return pl.ds(pl.multiple_of(b * ROWS, F), COLS)

    def outputs(b, ahead=0):
        return pl.ds(pl.multiple_of(b * ROWS + ahead * F, F), ROWS)

    def layer1(b, carry):
        pre = mixed(lhs_f.at[0], a1h[inputs(b), :], a1l[inputs(b), :], False)
        pre = pre + jnp.concatenate([bcol[1]] * OUT, axis=0)
        a, d = silu_parts(pre)
        a2h[outputs(b), :], a2l[outputs(b), :] = split(a)
        d1[outputs(b), :] = d
        return carry

    lax.fori_loop(0, NBLK, layer1, 0)

    @pl.when(me == 0)
    def _():
        clear(slice(0, F), (a2h, a2l, d1))

    @pl.when(me == nchan - 1)
    def _():
        clear(slice(65 * F, 66 * F), (a2h, a2l, d1))

    par = lax.rem(me, 2) * OWN

    def layer2(b, carry):
        ah, al = a2h[inputs(b), :], a2l[inputs(b), :]
        pre = mixed(lhs_f.at[1], ah, al, False)
        pre = pre + jnp.concatenate([bcol[2]] * OUT, axis=0)
        a, d = silu_parts(pre)
        head = bcol[3]
        heads = hacc[...]
        grads = []
        for k in range(OUT):
            at = slice(k * F, k * F + F)
            row = jnp.sum(head * a[at], axis=0, keepdims=True)
            outs[pl.ds(par + OUT * b + k, 1), :] = row
            spot = pl.ds(OUT * b + k + HALO, 1)
            g_out = jnp.where(OUT * b + k < OWN, coef[spot, :], 0.0) * (row - sig[spot, :])
            heads = heads + g_out * a[at]
            grads.append((head * d[at]) * g_out)
        hacc[...] = heads
        g = jnp.concatenate(grads, axis=0)
        g2h[outputs(b, 2), :], g2l[outputs(b, 2), :] = split(g)
        add_channels(bacc.at[2], g)
        acc[1] += dot_t(shifted_triple(g), jnp.concatenate([ah, ah, al], axis=1))
        return carry

    lax.fori_loop(0, NBLK, layer2, 0)

    out_ref[...] = outs[:128, :].T

    def back2(b, carry):
        g_act = mixed(lhs_b.at[1], g2h[inputs(b), :], g2l[inputs(b), :], True)
        g = g_act * d1[outputs(b), :]
        g1h[outputs(b, 2), :], g1l[outputs(b, 2), :] = split(g)
        add_channels(bacc.at[1], g)
        ah, al = a1h[inputs(b), :], a1l[inputs(b), :]
        acc[0] += dot_t(shifted_triple(g), jnp.concatenate([ah, ah, al], axis=1))
        return carry

    lax.fori_loop(0, NBLK, back2, 0)

    def back1(b, carry):
        g_act = mixed(lhs_b.at[0], g1h[inputs(b), :], g1l[inputs(b), :], True)
        g = g_act * d0[outputs(b), :]
        g0h[outputs(b), :], g0l[outputs(b), :] = split(g)
        add_channels(bacc.at[0], g)
        return carry

    lax.fori_loop(0, NBLK + 1, back1, 0)

    def grads0(b, carry):
        parts = columns(b)
        hi = jnp.concatenate([p[0] for p in parts], axis=0)
        lo = jnp.concatenate([p[1] for p in parts], axis=0)
        at = pl.ds(pl.multiple_of(b * 8 * F, F), 8 * F)
        gh, gl = g0h[at, :], g0l[at, :]
        left = jnp.concatenate([gh, gl, gh], axis=1)
        right = jnp.concatenate([hi, hi, lo], axis=1)
        acc0[...] += dot_t(left, right)
        return carry

    lax.fori_loop(0, 9, grads0, 0)

    ci = iota((F, COLS), 1) >> 5
    pack_rows = []
    pack_pw = []
    lane48 = iota((F, 48), 1)
    taps0 = []
    for tap in range(9):
        total = jnp.zeros((F, 48), F32)
        for co in range(8):
            here = lane48 == (tap % 3) * 16 + co + tap // 3
            total = total + jnp.where(here, acc0[co * F : co * F + F, :], 0.0)
        taps0.append(jnp.sum(total, axis=1, keepdims=True))
    grad_pw = jnp.zeros((F, F), F32)
    for tap in range(9):
        grad_pw = grad_pw + taps0[tap] * as_row(dw[0][:, tap : tap + 1])[:, :F]
        pack_rows.append(jnp.sum(taps0[tap] * pw[0], axis=0, keepdims=True))
    pack_pw.append(grad_pw)
    for l in (1, 2):
        wide = jnp.concatenate([pw[l]] * INN, axis=1)
        grad_pw = jnp.zeros((F, COLS), F32)
        for tap in range(9):
            i, j = tap // 3, tap % 3
            total = jnp.zeros((F, COLS), F32)
            for co in range(OUT):
                at = slice(j * ROWS + co * F, j * ROWS + co * F + F)
                total = total + jnp.where(ci == co + i, acc[l - 1, at, :], 0.0)
            grad_pw = grad_pw + total * as_row(dw[l][:, tap : tap + 1])
            pack_rows.append(fold(jnp.sum(total * wide, axis=0, keepdims=True)))
        pack_pw.append(fold(grad_pw))
    for l in range(3):
        pack_rows.append(as_row(jnp.sum(bacc[l], axis=1, keepdims=True))[:, :F])
    pack_rows.append(as_row(jnp.sum(hacc[...], axis=1, keepdims=True))[:, :F])
    pack_rows.append(jnp.zeros((1, F), F32))
    pack_pw.append(jnp.concatenate(pack_rows, axis=0))
    pack_ref[...] = jnp.concatenate(pack_pw, axis=1)


def comm_out(
    ntm, nchan, outt_ref, pack_ref, dw_out, pw_out, bias_out, head_out, den_out,
    got, r1, r2, r3, v1, v2, dsems, rsems,
):
    me, tm = lax.axis_index("chan"), lax.axis_index("tm")
    near = 8
    far = nchan // near
    barrier = pltpu.get_barrier_semaphore()

    def greet(k, carry):
        pl.semaphore_signal(
            barrier, inc=1, device_id={"chan": lax.rem(me + k, nchan)}, device_id_type=MESH
        )
        return carry

    def greet_tm(k, carry):
        pl.semaphore_signal(
            barrier, inc=1, device_id={"tm": lax.rem(tm + k, ntm)}, device_id_type=MESH
        )
        return carry

    lax.fori_loop(1, ntm, greet_tm, 0)
    lax.fori_loop(1, nchan, greet, 0)
    pl.semaphore_wait(barrier, nchan - 1 + ntm - 1)

    def stage(src, dst, slot, count, where, which):
        def go(k, carry):
            pltpu.make_async_remote_copy(
                src_ref=src,
                dst_ref=dst.at[slot],
                send_sem=rsems.at[which, 0],
                recv_sem=rsems.at[which, 1],
                device_id=where(k),
                device_id_type=MESH,
            ).start()
            return carry

        lax.fori_loop(1, count, go, 0)
        dst[slot] = src[...]

    def finish(dst, count, where, which):
        pltpu.make_async_remote_copy(
            src_ref=dst.at[pl.ds(0, count - 1)],
            dst_ref=dst.at[pl.ds(0, count - 1)],
            send_sem=rsems.at[which, 0],
            recv_sem=rsems.at[which, 1],
            device_id=where(1),
            device_id_type=MESH,
        ).wait()
        total = dst[0]
        for k in range(1, count):
            total = total + dst[k]
        return total

    def by_tm(k):
        return {"tm": lax.rem(tm + k, ntm)}

    base = (me // near) * near

    def by_near(k):
        return {"chan": base + lax.rem(me - base + k, near)}

    def by_far(k):
        return {"chan": lax.rem(me + near * k, nchan)}

    stage(pack_ref, r1, tm, ntm, by_tm, 0)

    def push(k, carry):
        peer = lax.rem(me + k, nchan)
        pltpu.make_async_remote_copy(
            src_ref=outt_ref.at[pl.ds(pl.multiple_of(peer * 8, 8), 8), :],
            dst_ref=got.at[pl.ds(pl.multiple_of(me * 8, 8), 8), :],
            send_sem=dsems.at[0],
            recv_sem=dsems.at[1],
            device_id={"chan": peer},
            device_id_type=MESH,
        ).start()
        return carry

    lax.fori_loop(1, nchan, push, 0)
    mine = pl.ds(pl.multiple_of(me * 8, 8), 8)
    got[mine, :] = outt_ref[mine, :]

    v1[...] = finish(r1, ntm, by_tm, 0)
    stage(v1, r2, me - base, near, by_near, 1)
    v2[...] = finish(r2, near, by_near, 1)
    stage(v2, r3, me // near, far, by_far, 2)

    rest = 8 * (nchan - 1)
    pltpu.make_async_remote_copy(
        src_ref=outt_ref.at[pl.ds(0, rest), :],
        dst_ref=got.at[pl.ds(0, rest), :],
        send_sem=dsems.at[0],
        recv_sem=dsems.at[1],
        device_id={"chan": lax.rem(me + 1, nchan)},
        device_id_type=MESH,
    ).wait()
    lane = iota((8, 128), 1)
    for k in range(nchan // 2):
        den_out[0, :, 128 * k : 128 * k + 128] = jnp.where(
            lane < OWN, got[16 * k : 16 * k + 8, :], got[16 * k + 8 : 16 * k + 16, :]
        )

    total = finish(r3, far, by_far, 2)
    for l in range(3):
        pw_out[l] = total[:, F * l : F * l + F]
    bias_out[...] = total[27:30, 96:128]
    head_out[...] = total[30:31, 96:128]
    padded = jnp.concatenate([total, jnp.zeros((96, 128), F32)], axis=0)
    turned = padded.T
    for l in range(3):
        dw_out[l] = turned[96:128, 9 * l : 9 * l + 9]


def vmem():
    return pl.BlockSpec(memory_space=pltpu.VMEM)


def on_device(ntm, nchan, recording, blind_mask, dw_kernels, pw_weights, biases, head_weights):
    sds = jax.ShapeDtypeStruct
    win, maskx = pl.pallas_call(
        functools.partial(comm_in, nchan),
        out_shape=(sds((T, 128), F32), sds((96, T), jnp.int32)),
        in_specs=[vmem()] * 2,
        out_specs=(vmem(), vmem()),
        scratch_shapes=[
            pltpu.VMEM((T, 128), F32),
            pltpu.SemaphoreType.DMA((2,)),
            pltpu.SemaphoreType.DMA((4,)),
        ],
        compiler_params=pltpu.CompilerParams(collective_id=0, has_side_effects=True),
        name="comm_in",
    )(recording, blind_mask)
    scale = SPOT_EVERY / (ntm * nchan * OWN * T)
    outt, pack = run_compute(
        nchan, scale, win, maskx, dw_kernels, pw_weights, biases, head_weights
    )
    dw_grad, pw_grad, bias_grad, head_grad, denoised = pl.pallas_call(
        functools.partial(comm_out, ntm, nchan),
        out_shape=(
            sds((3, F, 9), F32),
            sds((3, F, F), F32),
            sds((3, F), F32),
            sds((1, F), F32),
            sds((1, 8, OWN * nchan), F32),
        ),
        in_specs=[vmem()] * 2,
        out_specs=(vmem(),) * 5,
        scratch_shapes=[
            pltpu.VMEM((T, 128), F32),
            pltpu.VMEM((ntm, F, 128), F32),
            pltpu.VMEM((8, F, 128), F32),
            pltpu.VMEM((nchan // 8, F, 128), F32),
            pltpu.VMEM((F, 128), F32),
            pltpu.VMEM((F, 128), F32),
            pltpu.SemaphoreType.DMA((2,)),
            pltpu.SemaphoreType.DMA((3, 2)),
        ],
        compiler_params=pltpu.CompilerParams(collective_id=1, has_side_effects=True),
        name="comm_out",
    )(outt, pack)
    return dw_grad, pw_grad, bias_grad, head_grad.reshape(F), denoised


def run_compute(nchan, scale, win, maskx, dw_kernels, pw_weights, biases, head_weights):
    sds = jax.ShapeDtypeStruct
    return pl.pallas_call(
        functools.partial(compute, nchan, scale),
        out_shape=(sds((T, 128), F32), sds((F, 128), F32)),
        in_specs=[vmem()] * 6,
        out_specs=(vmem(), vmem()),
        scratch_shapes=[
            pltpu.VMEM((80, T), F32),
            pltpu.VMEM((80, T), F32),
            pltpu.VMEM((3, 80, T), F32),
            pltpu.VMEM((8 * F, 144), BF16),
            pltpu.VMEM((2, 3 * ROWS, 3 * COLS), BF16),
            pltpu.VMEM((2, 3 * ROWS, 3 * COLS), BF16),
            pltpu.VMEM((72 * F, T), BF16),
            pltpu.VMEM((72 * F, T), BF16),
            pltpu.VMEM((68 * F, T), BF16),
            pltpu.VMEM((68 * F, T), BF16),
            pltpu.VMEM((72 * F, T), F32),
            pltpu.VMEM((66 * F, T), F32),
            pltpu.VMEM((68 * F, T), BF16),
            pltpu.VMEM((68 * F, T), BF16),
            pltpu.VMEM((74 * F, T), BF16),
            pltpu.VMEM((74 * F, T), BF16),
            pltpu.VMEM((72 * F, T), BF16),
            pltpu.VMEM((72 * F, T), BF16),
            pltpu.VMEM((2, 3 * ROWS, COLS), F32),
            pltpu.VMEM((8 * F, 48), F32),
            pltpu.VMEM((3, F, T), F32),
            pltpu.VMEM((F, T), F32),
            pltpu.VMEM((4, F, T), F32),
            pltpu.VMEM((136, T), F32),
        ],
        compiler_params=pltpu.CompilerParams(vmem_limit_bytes=48 << 20),
        name="compute",
    )(win, maskx, dw_kernels, pw_weights, biases.T, head_weights.reshape(F, 1))


def solution(mesh):
    placed = (P("tm", "chan", None), P("tm", "chan", None), P(), P(), P(), P())
    return jax.shard_map(
        functools.partial(on_device, mesh.shape["tm"], mesh.shape["chan"]),
        mesh=mesh,
        in_specs=placed,
        out_specs=(P(), P(), P(), P(), P("tm", "chan", None)),
        check_vma=False,
    )
```

```python
import functools

import jax
import jax.numpy as jnp
from jax import lax
from jax.experimental import pallas as pl
from jax.experimental.pallas import tpu as pltpu
from jax.sharding import PartitionSpec as P

SPOT_EVERY = 8
F = 32
T = 256
OWN = 64
HALO = 3
OUT = 6
INN = 8
ROWS = OUT * F
COLS = INN * F
NBLK = 11
MESH = pl.DeviceIdType.MESH
F32 = jnp.float32
BF16 = jnp.bfloat16


def aligned(start, size):
    return start if isinstance(start, int) else pl.multiple_of(start, size)


def run(count, body):
    for b in range(count):
        body(b)


def iota(shape, dim):
    return lax.broadcasted_iota(jnp.int32, shape, dim)


def split(x):
    hi = x.astype(BF16)
    return hi, (x - hi.astype(F32)).astype(BF16)


def later(x):
    first = iota((x.shape[0], 128), 1) == 0
    a, b = pltpu.roll(x[:, :128], 1, 1), pltpu.roll(x[:, 128:], 1, 1)
    return jnp.concatenate([jnp.where(first, 0.0, a), jnp.where(first, a, b)], axis=1)


def earlier(x):
    last = iota((x.shape[0], 128), 1) == 127
    a, b = pltpu.roll(x[:, :128], 127, 1), pltpu.roll(x[:, 128:], 127, 1)
    return jnp.concatenate([jnp.where(last, b, a), jnp.where(last, 0.0, b)], axis=1)


def dot(a, b):
    return jnp.dot(a, b, preferred_element_type=F32)


def dot_t(a, b):
    return lax.dot_general(a, b, (((1,), (1,)), ((), ())), preferred_element_type=F32)


def as_row(column):
    same = iota((F, COLS), 0) == (iota((F, COLS), 1) & (F - 1))
    return jnp.sum(jnp.where(same, column, 0.0), axis=0, keepdims=True)


def fill_windows(rec_ref, send):
    lane = iota((8, 128), 1)
    tiles = rec_ref.shape[2] // 128
    zero = jnp.zeros((8, 128), F32)
    tile = [rec_ref[0, :, 128 * k : 128 * k + 128] for k in range(tiles)]
    for k in range(tiles):
        before = tile[k - 1] if k > 0 else zero
        after = tile[k + 1] if k < tiles - 1 else zero
        even = jnp.where(lane < HALO, pltpu.roll(before, HALO, 1), pltpu.roll(tile[k], HALO, 1))
        odd = jnp.where(
            lane < OWN + HALO,
            pltpu.roll(tile[k], OWN + HALO, 1),
            pltpu.roll(after, OWN + HALO, 1),
        )
        send[16 * k : 16 * k + 8, :] = even
        send[16 * k + 8 : 16 * k + 16, :] = odd


def comm_in(nchan, rec_ref, mask_ref, win_ref, maskx_ref, send, sems, bsems):
    me = lax.axis_index("chan")
    right, left = lax.rem(me + 1, nchan), lax.rem(me + nchan - 1, nchan)
    barrier = pltpu.get_barrier_semaphore()

    def greet(k, carry):
        pl.semaphore_signal(
            barrier, inc=1, device_id={"chan": lax.rem(me + k, nchan)}, device_id_type=MESH
        )
        return carry

    lax.fori_loop(1, nchan, greet, 0)
    fill_windows(rec_ref, send)
    pl.semaphore_wait(barrier, nchan - 1)

    def tile_copy(peer):
        return pltpu.make_async_remote_copy(
            src_ref=send.at[pl.ds(pl.multiple_of(peer * 8, 8), 8), :],
            dst_ref=win_ref.at[pl.ds(pl.multiple_of(me * 8, 8), 8), :],
            send_sem=sems.at[0],
            recv_sem=sems.at[1],
            device_id={"chan": peer},
            device_id_type=MESH,
        )

    to_right = pltpu.make_async_remote_copy(
        src_ref=mask_ref.at[0, pl.ds(OWN - 8, 8), :],
        dst_ref=maskx_ref.at[pl.ds(0, 8), :],
        send_sem=bsems.at[0],
        recv_sem=bsems.at[1],
        device_id={"chan": right},
        device_id_type=MESH,
    )
    to_left = pltpu.make_async_remote_copy(
        src_ref=mask_ref.at[0, pl.ds(0, 8), :],
        dst_ref=maskx_ref.at[pl.ds(OWN + 8, 8), :],
        send_sem=bsems.at[2],
        recv_sem=bsems.at[3],
        device_id={"chan": left},
        device_id_type=MESH,
    )
    to_right.start()
    to_left.start()

    def push(k, carry):
        tile_copy(lax.rem(me + k, nchan)).start()
        return carry

    lax.fori_loop(1, nchan, push, 0)
    mine = pl.ds(pl.multiple_of(me * 8, 8), 8)
    win_ref[mine, :] = send[mine, :]
    maskx_ref[8 : OWN + 8, :] = mask_ref[0]
    rest = 8 * (nchan - 1)
    every = pltpu.make_async_remote_copy(
        src_ref=send.at[pl.ds(0, rest), :],
        dst_ref=win_ref.at[pl.ds(0, rest), :],
        send_sem=sems.at[0],
        recv_sem=sems.at[1],
        device_id={"chan": right},
        device_id_type=MESH,
    )
    every.wait()
    to_right.wait()
    to_left.wait()


def forward_weights(lhs, pw, dw):
    wide = jnp.concatenate([pw] * INN, axis=1)
    ci = iota((F, COLS), 1) >> 5
    rows = [as_row(dw[:, tap : tap + 1]) for tap in range(9)]
    for j in range(3):
        for co in range(OUT):
            taps = jnp.zeros((F, COLS), F32)
            for i in range(3):
                taps = jnp.where(ci == co + i, rows[3 * i + j], taps)
            hi, lo = split(wide * taps)
            at = slice(j * ROWS + co * F, j * ROWS + co * F + F)
            lhs[at, 0:COLS] = hi
            lhs[at, COLS : 2 * COLS] = lo
            lhs[at, 2 * COLS : 3 * COLS] = hi


def backward_weights(lhs, pw_t, dw):
    wide = jnp.concatenate([pw_t] * INN, axis=1)
    ci = iota((F, COLS), 1) >> 5
    cols = [jnp.broadcast_to(dw[:, tap : tap + 1], (F, COLS)) for tap in range(9)]
    for j in range(3):
        for co in range(OUT):
            taps = jnp.zeros((F, COLS), F32)
            for i in range(3):
                taps = jnp.where(ci == co + 2 - i, cols[3 * i + j], taps)
            hi, lo = split(wide * taps)
            at = slice(j * ROWS + co * F, j * ROWS + co * F + F)
            lhs[at, 0:COLS] = hi
            lhs[at, COLS : 2 * COLS] = lo
            lhs[at, 2 * COLS : 3 * COLS] = hi


def first_weights(lhs, pw, dw):
    lane = iota((F, 144), 1)
    part = (lane >= 48).astype(jnp.int32) + (lane >= 96).astype(jnp.int32)
    spot = lane - 48 * part
    j_of, ci = spot >> 4, spot & 15
    cols = [
        jnp.sum(pw * as_row(dw[:, tap : tap + 1])[:, :F], axis=1, keepdims=True)
        for tap in range(9)
    ]
    for co in range(8):
        taps = jnp.zeros((F, 144), F32)
        for tap in range(9):
            here = (ci == co + tap // 3) & (j_of == tap % 3)
            taps = jnp.where(here, cols[tap], taps)
        hi = taps.astype(BF16).astype(F32)
        lhs[co * F : co * F + F, :] = jnp.where(part == 1, taps - hi, hi).astype(BF16)


def tripled(hi, lo):
    return jnp.concatenate([hi, hi, lo], axis=0)


def silu_parts(pre):
    s = 0.5 * jnp.tanh(0.5 * pre) + 0.5
    a = pre * s
    return a, s + (a - a * s)


def mixed(lhs, hi, lo, flip):
    prod = dot(lhs[...], tripled(hi, lo))
    first, mid, last = prod[:ROWS], prod[ROWS : 2 * ROWS], prod[2 * ROWS :]
    if flip:
        first, last = last, first
    return mid + later(first) + earlier(last)


def fold(x):
    y = x[:, :128] + x[:, 128:]
    y = y + pltpu.roll(y, 64, 1)
    y = y + pltpu.roll(y, 32, 1)
    return y[:, :F]


def shifted_triple(g):
    hi, lo = split(g)
    parts = []
    for move in (earlier, lambda x: x, later):
        a, b = move(hi), move(lo)
        parts.append(jnp.concatenate([a, b, a], axis=1))
    return jnp.concatenate(parts, axis=0)


def add_channels(acc, g):
    total = acc[...]
    for k in range(OUT):
        total = total + g[k * F : k * F + F]
    acc[...] = total


def compute(
    nchan, scale, win_ref, maskx_ref, dw_ref, pw_ref, bias_ref, head_ref, out_ref, pack_ref,
    sig, coef, wins, lhs0, lhs_f, lhs_b, a1h, a1l, a2h, a2l, d0, d1,
    g2h, g2l, g1h, g1l, g0h, g0l, acc, acc0, bacc, hacc, bcol, outs,
):
    me = lax.axis_index("chan")
    dw = [dw_ref[l] for l in range(3)]
    pw = [pw_ref[l] for l in range(3)]

    first_weights(lhs0, pw[0], dw[0])
    for l in (1, 2):
        forward_weights(lhs_f.at[l - 1], pw[l], dw[l])
        backward_weights(lhs_b.at[l - 1], pw[l].T, dw[l])
    for l in range(3):
        bcol[l] = jnp.broadcast_to(bias_ref[:, l : l + 1], (F, T))
    bcol[3] = jnp.broadcast_to(head_ref[...], (F, T))

    turned = win_ref[...].T
    sig[...] = turned[:80]
    blind = maskx_ref[5:85, :] == 1
    coef[...] = jnp.where(blind, 2.0 * scale, 0.0)
    act0 = jnp.where(blind, 0.0, turned[:80])
    wins[0] = later(act0)
    wins[1] = act0
    wins[2] = earlier(act0)

    zero2 = jnp.zeros((2 * F, T), BF16)
    for ref in (g2h, g2l, g1h, g1l):
        ref[: 2 * F, :] = zero2
    for ref in (g1h, g1l):
        ref[68 * F :, :] = jnp.zeros((6 * F, T), BF16)
    for ref in (a2h, a2l):
        ref[66 * F :, :] = zero2
    acc[...] = jnp.zeros_like(acc)
    acc0[...] = jnp.zeros_like(acc0)
    bacc[...] = jnp.zeros_like(bacc)
    hacc[...] = jnp.zeros_like(hacc)
    outs[...] = jnp.zeros_like(outs)

    def columns(b):
        return [split(wins[j, pl.ds(aligned(8 * b, 8), 16), :]) for j in range(3)]

    def layer0(b):
        parts = columns(b)
        hi = jnp.concatenate([p[0] for p in parts], axis=0)
        lo = jnp.concatenate([p[1] for p in parts], axis=0)
        pre = dot(lhs0[...], tripled(hi, lo))
        pre = pre + jnp.concatenate([bcol[0]] * 8, axis=0)
        a, d = silu_parts(pre)
        at = pl.ds(aligned(b * 8 * F, F), 8 * F)
        a1h[at, :], a1l[at, :] = split(a)
        d0[at, :] = d

    run(9, layer0)

    def clear(ends, refs):
        for ref in refs:
            ref[ends, :] = jnp.zeros(((ends.stop - ends.start), T), ref.dtype)

    @pl.when(me == 0)
    def _():
        clear(slice(0, 2 * F), (a1h, a1l, d0))

    @pl.when(me == nchan - 1)
    def _():
        clear(slice(66 * F, 68 * F), (a1h, a1l, d0))

    def inputs(b):
        return pl.ds(aligned(b * ROWS, F), COLS)

    def outputs(b, ahead=0):
        return pl.ds(aligned(b * ROWS + ahead * F, F), ROWS)

    def layer1(b):
        pre = mixed(lhs_f.at[0], a1h[inputs(b), :], a1l[inputs(b), :], False)
        pre = pre + jnp.concatenate([bcol[1]] * OUT, axis=0)
        a, d = silu_parts(pre)
        a2h[outputs(b), :], a2l[outputs(b), :] = split(a)
        d1[outputs(b), :] = d

    run(NBLK, layer1)

    @pl.when(me == 0)
    def _():
        clear(slice(0, F), (a2h, a2l, d1))

    @pl.when(me == nchan - 1)
    def _():
        clear(slice(65 * F, 66 * F), (a2h, a2l, d1))

    par = lax.rem(me, 2) * OWN

    def layer2(b):
        ah, al = a2h[inputs(b), :], a2l[inputs(b), :]
        pre = mixed(lhs_f.at[1], ah, al, False)
        pre = pre + jnp.concatenate([bcol[2]] * OUT, axis=0)
        a, d = silu_parts(pre)
        head = bcol[3]
        heads = hacc[...]
        grads = []
        for k in range(OUT):
            at = slice(k * F, k * F + F)
            row = jnp.sum(head * a[at], axis=0, keepdims=True)
            outs[pl.ds(par + OUT * b + k, 1), :] = row
            spot = pl.ds(OUT * b + k + HALO, 1)
            g_out = jnp.where(OUT * b + k < OWN, coef[spot, :], 0.0) * (row - sig[spot, :])
            heads = heads + g_out * a[at]
            grads.append((head * d[at]) * g_out)
        hacc[...] = heads
        g = jnp.concatenate(grads, axis=0)
        g2h[outputs(b, 2), :], g2l[outputs(b, 2), :] = split(g)
        add_channels(bacc.at[2], g)
        acc[1] += dot_t(shifted_triple(g), jnp.concatenate([ah, ah, al], axis=1))

    run(NBLK, layer2)

    out_ref[...] = outs[:128, :].T

    def back2(b):
        g_act = mixed(lhs_b.at[1], g2h[inputs(b), :], g2l[inputs(b), :], True)
        g = g_act * d1[outputs(b), :]
        g1h[outputs(b, 2), :], g1l[outputs(b, 2), :] = split(g)
        add_channels(bacc.at[1], g)
        ah, al = a1h[inputs(b), :], a1l[inputs(b), :]
        acc[0] += dot_t(shifted_triple(g), jnp.concatenate([ah, ah, al], axis=1))

    run(NBLK, back2)

    def back1(b):
        g_act = mixed(lhs_b.at[0], g1h[inputs(b), :], g1l[inputs(b), :], True)
        g = g_act * d0[outputs(b), :]
        g0h[outputs(b), :], g0l[outputs(b), :] = split(g)
        add_channels(bacc.at[0], g)

    run(NBLK + 1, back1)

    def grads0(b):
        parts = columns(b)
        hi = jnp.concatenate([p[0] for p in parts], axis=0)
        lo = jnp.concatenate([p[1] for p in parts], axis=0)
        at = pl.ds(aligned(b * 8 * F, F), 8 * F)
        gh, gl = g0h[at, :], g0l[at, :]
        left = jnp.concatenate([gh, gl, gh], axis=1)
        right = jnp.concatenate([hi, hi, lo], axis=1)
        acc0[...] += dot_t(left, right)

    run(9, grads0)

    ci = iota((F, COLS), 1) >> 5
    pack_rows = []
    pack_pw = []
    lane48 = iota((F, 48), 1)
    taps0 = []
    for tap in range(9):
        total = jnp.zeros((F, 48), F32)
        for co in range(8):
            here = lane48 == (tap % 3) * 16 + co + tap // 3
            total = total + jnp.where(here, acc0[co * F : co * F + F, :], 0.0)
        taps0.append(jnp.sum(total, axis=1, keepdims=True))
    grad_pw = jnp.zeros((F, F), F32)
    for tap in range(9):
        grad_pw = grad_pw + taps0[tap] * as_row(dw[0][:, tap : tap + 1])[:, :F]
        pack_rows.append(jnp.sum(taps0[tap] * pw[0], axis=0, keepdims=True))
    pack_pw.append(grad_pw)
    for l in (1, 2):
        wide = jnp.concatenate([pw[l]] * INN, axis=1)
        grad_pw = jnp.zeros((F, COLS), F32)
        for tap in range(9):
            i, j = tap // 3, tap % 3
            total = jnp.zeros((F, COLS), F32)
            for co in range(OUT):
                at = slice(j * ROWS + co * F, j * ROWS + co * F + F)
                total = total + jnp.where(ci == co + i, acc[l - 1, at, :], 0.0)
            grad_pw = grad_pw + total * as_row(dw[l][:, tap : tap + 1])
            pack_rows.append(fold(jnp.sum(total * wide, axis=0, keepdims=True)))
        pack_pw.append(fold(grad_pw))
    for l in range(3):
        pack_rows.append(as_row(jnp.sum(bacc[l], axis=1, keepdims=True))[:, :F])
    pack_rows.append(as_row(jnp.sum(hacc[...], axis=1, keepdims=True))[:, :F])
    pack_rows.append(jnp.zeros((1, F), F32))
    pack_pw.append(jnp.concatenate(pack_rows, axis=0))
    pack_ref[...] = jnp.concatenate(pack_pw, axis=1)


def comm_out(
    ntm, nchan, outt_ref, pack_ref, dw_out, pw_out, bias_out, head_out, den_out,
    got, r1, r2, r3, v1, v2, dsems, rsems,
):
    me, tm = lax.axis_index("chan"), lax.axis_index("tm")
    near = 8
    far = nchan // near
    barrier = pltpu.get_barrier_semaphore()

    def greet(k, carry):
        pl.semaphore_signal(
            barrier, inc=1, device_id={"chan": lax.rem(me + k, nchan)}, device_id_type=MESH
        )
        return carry

    def greet_tm(k, carry):
        pl.semaphore_signal(
            barrier, inc=1, device_id={"tm": lax.rem(tm + k, ntm)}, device_id_type=MESH
        )
        return carry

    lax.fori_loop(1, ntm, greet_tm, 0)
    lax.fori_loop(1, nchan, greet, 0)
    pl.semaphore_wait(barrier, nchan - 1 + ntm - 1)

    def stage(src, dst, slot, count, where, which):
        def go(k, carry):
            pltpu.make_async_remote_copy(
                src_ref=src,
                dst_ref=dst.at[slot],
                send_sem=rsems.at[which, 0],
                recv_sem=rsems.at[which, 1],
                device_id=where(k),
                device_id_type=MESH,
            ).start()
            return carry

        lax.fori_loop(1, count, go, 0)
        dst[slot] = src[...]

    def finish(dst, count, where, which):
        pltpu.make_async_remote_copy(
            src_ref=dst.at[pl.ds(0, count - 1)],
            dst_ref=dst.at[pl.ds(0, count - 1)],
            send_sem=rsems.at[which, 0],
            recv_sem=rsems.at[which, 1],
            device_id=where(1),
            device_id_type=MESH,
        ).wait()
        total = dst[0]
        for k in range(1, count):
            total = total + dst[k]
        return total

    def by_tm(k):
        return {"tm": lax.rem(tm + k, ntm)}

    base = (me // near) * near

    def by_near(k):
        return {"chan": base + lax.rem(me - base + k, near)}

    def by_far(k):
        return {"chan": lax.rem(me + near * k, nchan)}

    stage(pack_ref, r1, tm, ntm, by_tm, 0)

    def push(k, carry):
        peer = lax.rem(me + k, nchan)
        pltpu.make_async_remote_copy(
            src_ref=outt_ref.at[pl.ds(pl.multiple_of(peer * 8, 8), 8), :],
            dst_ref=got.at[pl.ds(pl.multiple_of(me * 8, 8), 8), :],
            send_sem=dsems.at[0],
            recv_sem=dsems.at[1],
            device_id={"chan": peer},
            device_id_type=MESH,
        ).start()
        return carry

    lax.fori_loop(1, nchan, push, 0)
    mine = pl.ds(pl.multiple_of(me * 8, 8), 8)
    got[mine, :] = outt_ref[mine, :]

    v1[...] = finish(r1, ntm, by_tm, 0)
    stage(v1, r2, me - base, near, by_near, 1)
    v2[...] = finish(r2, near, by_near, 1)
    stage(v2, r3, me // near, far, by_far, 2)

    rest = 8 * (nchan - 1)
    pltpu.make_async_remote_copy(
        src_ref=outt_ref.at[pl.ds(0, rest), :],
        dst_ref=got.at[pl.ds(0, rest), :],
        send_sem=dsems.at[0],
        recv_sem=dsems.at[1],
        device_id={"chan": lax.rem(me + 1, nchan)},
        device_id_type=MESH,
    ).wait()
    lane = iota((8, 128), 1)
    for k in range(nchan // 2):
        den_out[0, :, 128 * k : 128 * k + 128] = jnp.where(
            lane < OWN, got[16 * k : 16 * k + 8, :], got[16 * k + 8 : 16 * k + 16, :]
        )

    total = finish(r3, far, by_far, 2)
    for l in range(3):
        pw_out[l] = total[:, F * l : F * l + F]
    bias_out[...] = total[27:30, 96:128]
    head_out[...] = total[30:31, 96:128]
    padded = jnp.concatenate([total, jnp.zeros((96, 128), F32)], axis=0)
    turned = padded.T
    for l in range(3):
        dw_out[l] = turned[96:128, 9 * l : 9 * l + 9]


def vmem():
    return pl.BlockSpec(memory_space=pltpu.VMEM)


def on_device(ntm, nchan, recording, blind_mask, dw_kernels, pw_weights, biases, head_weights):
    sds = jax.ShapeDtypeStruct
    win, maskx = pl.pallas_call(
        functools.partial(comm_in, nchan),
        out_shape=(sds((T, 128), F32), sds((96, T), jnp.int32)),
        in_specs=[vmem()] * 2,
        out_specs=(vmem(), vmem()),
        scratch_shapes=[
            pltpu.VMEM((T, 128), F32),
            pltpu.SemaphoreType.DMA((2,)),
            pltpu.SemaphoreType.DMA((4,)),
        ],
        compiler_params=pltpu.CompilerParams(collective_id=0, has_side_effects=True),
        name="comm_in",
    )(recording, blind_mask)
    scale = SPOT_EVERY / (ntm * nchan * OWN * T)
    outt, pack = run_compute(
        nchan, scale, win, maskx, dw_kernels, pw_weights, biases, head_weights
    )
    dw_grad, pw_grad, bias_grad, head_grad, denoised = pl.pallas_call(
        functools.partial(comm_out, ntm, nchan),
        out_shape=(
            sds((3, F, 9), F32),
            sds((3, F, F), F32),
            sds((3, F), F32),
            sds((1, F), F32),
            sds((1, 8, OWN * nchan), F32),
        ),
        in_specs=[vmem()] * 2,
        out_specs=(vmem(),) * 5,
        scratch_shapes=[
            pltpu.VMEM((T, 128), F32),
            pltpu.VMEM((ntm, F, 128), F32),
            pltpu.VMEM((8, F, 128), F32),
            pltpu.VMEM((nchan // 8, F, 128), F32),
            pltpu.VMEM((F, 128), F32),
            pltpu.VMEM((F, 128), F32),
            pltpu.SemaphoreType.DMA((2,)),
            pltpu.SemaphoreType.DMA((3, 2)),
        ],
        compiler_params=pltpu.CompilerParams(collective_id=1, has_side_effects=True),
        name="comm_out",
    )(outt, pack)
    return dw_grad, pw_grad, bias_grad, head_grad.reshape(F), denoised


def run_compute(nchan, scale, win, maskx, dw_kernels, pw_weights, biases, head_weights):
    sds = jax.ShapeDtypeStruct
    return pl.pallas_call(
        functools.partial(compute, nchan, scale),
        out_shape=(sds((T, 128), F32), sds((F, 128), F32)),
        in_specs=[vmem()] * 6,
        out_specs=(vmem(), vmem()),
        scratch_shapes=[
            pltpu.VMEM((80, T), F32),
            pltpu.VMEM((80, T), F32),
            pltpu.VMEM((3, 80, T), F32),
            pltpu.VMEM((8 * F, 144), BF16),
            pltpu.VMEM((2, 3 * ROWS, 3 * COLS), BF16),
            pltpu.VMEM((2, 3 * ROWS, 3 * COLS), BF16),
            pltpu.VMEM((72 * F, T), BF16),
            pltpu.VMEM((72 * F, T), BF16),
            pltpu.VMEM((68 * F, T), BF16),
            pltpu.VMEM((68 * F, T), BF16),
            pltpu.VMEM((72 * F, T), F32),
            pltpu.VMEM((66 * F, T), F32),
            pltpu.VMEM((68 * F, T), BF16),
            pltpu.VMEM((68 * F, T), BF16),
            pltpu.VMEM((74 * F, T), BF16),
            pltpu.VMEM((74 * F, T), BF16),
            pltpu.VMEM((72 * F, T), BF16),
            pltpu.VMEM((72 * F, T), BF16),
            pltpu.VMEM((2, 3 * ROWS, COLS), F32),
            pltpu.VMEM((8 * F, 48), F32),
            pltpu.VMEM((3, F, T), F32),
            pltpu.VMEM((F, T), F32),
            pltpu.VMEM((4, F, T), F32),
            pltpu.VMEM((136, T), F32),
        ],
        compiler_params=pltpu.CompilerParams(vmem_limit_bytes=48 << 20),
        name="compute",
    )(win, maskx, dw_kernels, pw_weights, biases.T, head_weights.reshape(F, 1))


def solution(mesh):
    placed = (P("tm", "chan", None), P("tm", "chan", None), P(), P(), P(), P())
    return jax.shard_map(
        functools.partial(on_device, mesh.shape["tm"], mesh.shape["chan"]),
        mesh=mesh,
        in_specs=placed,
        out_specs=(P(), P(), P(), P(), P("tm", "chan", None)),
        check_vma=False,
    )
```

```python
import functools

import jax
import jax.numpy as jnp
from jax import lax
from jax.experimental import pallas as pl
from jax.experimental.pallas import tpu as pltpu
from jax.sharding import PartitionSpec as P

SPOT_EVERY = 8
F = 32
T = 256
OWN = 64
HALO = 3
OUT = 6
INN = 8
ROWS = OUT * F
COLS = INN * F
NBLK = 11
MESH = pl.DeviceIdType.MESH
F32 = jnp.float32
BF16 = jnp.bfloat16


def aligned(start, size):
    return start if isinstance(start, int) else pl.multiple_of(start, size)


def run(count, body):
    for b in range(count):
        body(b)


def iota(shape, dim):
    return lax.broadcasted_iota(jnp.int32, shape, dim)


def split(x):
    hi = x.astype(BF16)
    return hi, (x - hi.astype(F32)).astype(BF16)


def later(x):
    first = iota((x.shape[0], 128), 1) == 0
    a, b = pltpu.roll(x[:, :128], 1, 1), pltpu.roll(x[:, 128:], 1, 1)
    return jnp.concatenate([jnp.where(first, 0.0, a), jnp.where(first, a, b)], axis=1)


def earlier(x):
    last = iota((x.shape[0], 128), 1) == 127
    a, b = pltpu.roll(x[:, :128], 127, 1), pltpu.roll(x[:, 128:], 127, 1)
    return jnp.concatenate([jnp.where(last, b, a), jnp.where(last, 0.0, b)], axis=1)


def dot(a, b):
    return jnp.dot(a, b, preferred_element_type=F32)


def dot_t(a, b):
    return lax.dot_general(a, b, (((1,), (1,)), ((), ())), preferred_element_type=F32)


def repeated(row):
    return jnp.concatenate([row] * INN, axis=1)


def as_column(row):
    return jnp.sum(jnp.where(iota((F, F), 0) == iota((F, F), 1), row, 0.0), axis=1, keepdims=True)


def as_row(column):
    same = iota((F, COLS), 0) == (iota((F, COLS), 1) & (F - 1))
    return jnp.sum(jnp.where(same, column, 0.0), axis=0, keepdims=True)


def fill_windows(rec_ref, send):
    lane = iota((8, 128), 1)
    tiles = rec_ref.shape[2] // 128
    zero = jnp.zeros((8, 128), F32)
    tile = [rec_ref[0, :, 128 * k : 128 * k + 128] for k in range(tiles)]
    for k in range(tiles):
        before = tile[k - 1] if k > 0 else zero
        after = tile[k + 1] if k < tiles - 1 else zero
        even = jnp.where(lane < HALO, pltpu.roll(before, HALO, 1), pltpu.roll(tile[k], HALO, 1))
        odd = jnp.where(
            lane < OWN + HALO,
            pltpu.roll(tile[k], OWN + HALO, 1),
            pltpu.roll(after, OWN + HALO, 1),
        )
        send[16 * k : 16 * k + 8, :] = even
        send[16 * k + 8 : 16 * k + 16, :] = odd


def forward_weights(lhs, pw, dw):
    wide = jnp.concatenate([pw] * INN, axis=1)
    ci = iota((F, COLS), 1) >> 5
    rows = [repeated(row) for row in dw]
    for j in range(3):
        for co in range(OUT):
            taps = jnp.zeros((F, COLS), F32)
            for i in range(3):
                taps = jnp.where(ci == co + i, rows[3 * i + j], taps)
            hi, lo = split(wide * taps)
            at = slice(j * ROWS + co * F, j * ROWS + co * F + F)
            lhs[at, 0:COLS] = hi
            lhs[at, COLS : 2 * COLS] = lo
            lhs[at, 2 * COLS : 3 * COLS] = hi


def backward_weights(lhs, pw_t, dw):
    wide = jnp.concatenate([pw_t] * INN, axis=1)
    ci = iota((F, COLS), 1) >> 5
    cols = [jnp.broadcast_to(as_column(row), (F, COLS)) for row in dw]
    for j in range(3):
        for co in range(OUT):
            taps = jnp.zeros((F, COLS), F32)
            for i in range(3):
                taps = jnp.where(ci == co + 2 - i, cols[3 * i + j], taps)
            hi, lo = split(wide * taps)
            at = slice(j * ROWS + co * F, j * ROWS + co * F + F)
            lhs[at, 0:COLS] = hi
            lhs[at, COLS : 2 * COLS] = lo
            lhs[at, 2 * COLS : 3 * COLS] = hi


def first_weights(lhs, pw, dw):
    lane = iota((F, 144), 1)
    part = (lane >= 48).astype(jnp.int32) + (lane >= 96).astype(jnp.int32)
    spot = lane - 48 * part
    j_of, ci = spot >> 4, spot & 15
    cols = [jnp.sum(pw * row, axis=1, keepdims=True) for row in dw]
    for co in range(8):
        taps = jnp.zeros((F, 144), F32)
        for tap in range(9):
            here = (ci == co + tap // 3) & (j_of == tap % 3)
            taps = jnp.where(here, cols[tap], taps)
        hi = taps.astype(BF16).astype(F32)
        lhs[co * F : co * F + F, :] = jnp.where(part == 1, taps - hi, hi).astype(BF16)


def tripled(hi, lo):
    return jnp.concatenate([hi, hi, lo], axis=0)


def silu_parts(pre):
    s = 0.5 * jnp.tanh(0.5 * pre) + 0.5
    a = pre * s
    return a, s + (a - a * s)


def mixed(lhs, hi, lo, flip):
    prod = dot(lhs[...], tripled(hi, lo))
    first, mid, last = prod[:ROWS], prod[ROWS : 2 * ROWS], prod[2 * ROWS :]
    if flip:
        first, last = last, first
    return mid + later(first) + earlier(last)


def fold(x):
    y = x[:, :128] + x[:, 128:]
    y = y + pltpu.roll(y, 64, 1)
    y = y + pltpu.roll(y, 32, 1)
    return y[:, :F]


def shifted_triple(g):
    hi, lo = split(g)
    parts = []
    for move in (earlier, lambda x: x, later):
        a, b = move(hi), move(lo)
        parts.append(jnp.concatenate([a, b, a], axis=1))
    return jnp.concatenate(parts, axis=0)


def add_channels(acc, g):
    total = acc[...]
    for k in range(OUT):
        total = total + g[k * F : k * F + F]
    acc[...] = total


def step(
    ntm, nchan, scale,
    rec_ref, mask_ref, dw_ref, pw_ref, bias_ref, head_ref,
    dw_out, pw_out, bias_out, head_out, den_out,
    sig, coef, wins, lhs0, lhs_f, lhs_b, a1h, a1l, a2h, a2l, d0, d1,
    g2h, g2l, g1h, g1l, g0h, g0l, acc, acc0, bacc, hacc, bcol, outs,
    send, win, maskx, outt, got, pack, r1, v1, r2, v2, r3, sems,
):
    me, tm = lax.axis_index("chan"), lax.axis_index("tm")
    right, left = lax.rem(me + 1, nchan), lax.rem(me + nchan - 1, nchan)
    barrier = pltpu.get_barrier_semaphore()

    def chan_peer(k):
        return {"chan": lax.rem(me + k, nchan)}

    def tm_peer(k):
        return {"tm": lax.rem(tm + k, ntm)}

    def each(count, go):
        def body(k, carry):
            go(k)
            return carry

        lax.fori_loop(1, count, body, 0)

    def greet(where):
        pl.semaphore_signal(barrier, inc=1, device_id=where, device_id_type=MESH)

    def remote(src, dst, pair, where):
        return pltpu.make_async_remote_copy(
            src_ref=src,
            dst_ref=dst,
            send_sem=sems.at[2 * pair],
            recv_sem=sems.at[2 * pair + 1],
            device_id=where,
            device_id_type=MESH,
        )

    def rows8(index):
        return pl.ds(pl.multiple_of(index * 8, 8), 8)

    def arrived(dst, count, pair, where):
        remote(dst.at[pl.ds(0, count)], dst.at[pl.ds(0, count)], pair, where).wait()

    each(nchan, lambda k: greet(chan_peer(k)))
    each(ntm, lambda k: greet(tm_peer(k)))
    fill_windows(rec_ref, send)
    pl.semaphore_wait(barrier, nchan - 1 + ntm - 1)

    to_right = remote(
        mask_ref.at[0, pl.ds(OWN - 8, 8), :], maskx.at[pl.ds(0, 8), :], 0, {"chan": right}
    )
    to_left = remote(
        mask_ref.at[0, pl.ds(0, 8), :], maskx.at[pl.ds(OWN + 8, 8), :], 1, {"chan": left}
    )

    def push_in(k):
        peer = lax.rem(me + k, nchan)
        remote(send.at[rows8(peer), :], win.at[rows8(me), :], 2, {"chan": peer}).start()

    each(nchan, push_in)
    to_right.start()
    to_left.start()
    win[rows8(me), :] = send[rows8(me), :]
    maskx[8 : OWN + 8, :] = mask_ref[0]
    maskx[OWN + 16 :, :] = jnp.zeros((16, T), jnp.int32)

    dw = [[dw_ref[tap, l : l + 1, :] for tap in range(9)] for l in range(3)]
    pw = [pw_ref[l] for l in range(3)]
    first_weights(lhs0, pw[0], dw[0])
    for l in (1, 2):
        forward_weights(lhs_f.at[l - 1], pw[l], dw[l])
        backward_weights(lhs_b.at[l - 1], pw[l].T, dw[l])
    for l in range(3):
        bcol[l] = jnp.broadcast_to(as_column(bias_ref[l : l + 1, :]), (F, T))
    bcol[3] = jnp.broadcast_to(as_column(head_ref[...]), (F, T))

    zero2 = jnp.zeros((2 * F, T), BF16)
    for ref in (g2h, g2l, g1h, g1l):
        ref[: 2 * F, :] = zero2
    for ref in (g1h, g1l):
        ref[68 * F :, :] = jnp.zeros((6 * F, T), BF16)
    for ref in (a2h, a2l):
        ref[66 * F :, :] = zero2
    acc[...] = jnp.zeros_like(acc)
    acc0[...] = jnp.zeros_like(acc0)
    bacc[...] = jnp.zeros_like(bacc)
    hacc[...] = jnp.zeros_like(hacc)
    outs[...] = jnp.zeros_like(outs)

    to_right.wait()
    to_left.wait()
    arrived(win, 8 * (nchan - 1), 2, {"chan": right})
    turned = win[...].T
    sig[...] = turned[:80]
    blind = maskx[5:85, :] == 1
    coef[...] = jnp.where(blind, 2.0 * scale, 0.0)
    act0 = jnp.where(blind, 0.0, turned[:80])
    wins[0] = later(act0)
    wins[1] = act0
    wins[2] = earlier(act0)

    def columns(b):
        return [split(wins[j, pl.ds(aligned(8 * b, 8), 16), :]) for j in range(3)]

    def layer0(b):
        parts = columns(b)
        hi = jnp.concatenate([p[0] for p in parts], axis=0)
        lo = jnp.concatenate([p[1] for p in parts], axis=0)
        pre = dot(lhs0[...], tripled(hi, lo))
        pre = pre + jnp.concatenate([bcol[0]] * 8, axis=0)
        a, d = silu_parts(pre)
        at = pl.ds(aligned(b * 8 * F, F), 8 * F)
        a1h[at, :], a1l[at, :] = split(a)
        d0[at, :] = d

    run(9, layer0)

    def clear(ends, refs):
        for ref in refs:
            ref[ends, :] = jnp.zeros(((ends.stop - ends.start), T), ref.dtype)

    @pl.when(me == 0)
    def _():
        clear(slice(0, 2 * F), (a1h, a1l, d0))

    @pl.when(me == nchan - 1)
    def _():
        clear(slice(66 * F, 68 * F), (a1h, a1l, d0))

    def inputs(b):
        return pl.ds(aligned(b * ROWS, F), COLS)

    def outputs(b, ahead=0):
        return pl.ds(aligned(b * ROWS + ahead * F, F), ROWS)

    def layer1(b):
        pre = mixed(lhs_f.at[0], a1h[inputs(b), :], a1l[inputs(b), :], False)
        pre = pre + jnp.concatenate([bcol[1]] * OUT, axis=0)
        a, d = silu_parts(pre)
        a2h[outputs(b), :], a2l[outputs(b), :] = split(a)
        d1[outputs(b), :] = d

    run(NBLK, layer1)

    @pl.when(me == 0)
    def _():
        clear(slice(0, F), (a2h, a2l, d1))

    @pl.when(me == nchan - 1)
    def _():
        clear(slice(65 * F, 66 * F), (a2h, a2l, d1))

    par = lax.rem(me, 2) * OWN

    def layer2(b):
        ah, al = a2h[inputs(b), :], a2l[inputs(b), :]
        pre = mixed(lhs_f.at[1], ah, al, False)
        pre = pre + jnp.concatenate([bcol[2]] * OUT, axis=0)
        a, d = silu_parts(pre)
        head = bcol[3]
        heads = hacc[...]
        grads = []
        for k in range(OUT):
            at = slice(k * F, k * F + F)
            row = jnp.sum(head * a[at], axis=0, keepdims=True)
            outs[pl.ds(par + OUT * b + k, 1), :] = row
            spot = pl.ds(OUT * b + k + HALO, 1)
            g_out = jnp.where(OUT * b + k < OWN, coef[spot, :], 0.0) * (row - sig[spot, :])
            heads = heads + g_out * a[at]
            grads.append((head * d[at]) * g_out)
        hacc[...] = heads
        g = jnp.concatenate(grads, axis=0)
        g2h[outputs(b, 2), :], g2l[outputs(b, 2), :] = split(g)
        add_channels(bacc.at[2], g)
        acc[1] += dot_t(shifted_triple(g), jnp.concatenate([ah, ah, al], axis=1))

    run(NBLK, layer2)

    outt[...] = outs[:128, :].T

    def back2(b):
        g_act = mixed(lhs_b.at[1], g2h[inputs(b), :], g2l[inputs(b), :], True)
        g = g_act * d1[outputs(b), :]
        g1h[outputs(b, 2), :], g1l[outputs(b, 2), :] = split(g)
        add_channels(bacc.at[1], g)
        ah, al = a1h[inputs(b), :], a1l[inputs(b), :]
        acc[0] += dot_t(shifted_triple(g), jnp.concatenate([ah, ah, al], axis=1))

    run(NBLK, back2)

    def back1(b):
        g_act = mixed(lhs_b.at[0], g1h[inputs(b), :], g1l[inputs(b), :], True)
        g = g_act * d0[outputs(b), :]
        g0h[outputs(b), :], g0l[outputs(b), :] = split(g)
        add_channels(bacc.at[0], g)

    run(NBLK + 1, back1)

    def grads0(b):
        parts = columns(b)
        hi = jnp.concatenate([p[0] for p in parts], axis=0)
        lo = jnp.concatenate([p[1] for p in parts], axis=0)
        at = pl.ds(aligned(b * 8 * F, F), 8 * F)
        gh, gl = g0h[at, :], g0l[at, :]
        left = jnp.concatenate([gh, gl, gh], axis=1)
        right = jnp.concatenate([hi, hi, lo], axis=1)
        acc0[...] += dot_t(left, right)

    run(9, grads0)

    ci = iota((F, COLS), 1) >> 5
    taps_of = []
    pack_pw = []
    lane48 = iota((F, 48), 1)
    taps0 = []
    for tap in range(9):
        total = jnp.zeros((F, 48), F32)
        for co in range(8):
            here = lane48 == (tap % 3) * 16 + co + tap // 3
            total = total + jnp.where(here, acc0[co * F : co * F + F, :], 0.0)
        taps0.append(jnp.sum(total, axis=1, keepdims=True))
    grad_pw = jnp.zeros((F, F), F32)
    for tap in range(9):
        grad_pw = grad_pw + taps0[tap] * dw[0][tap]
        taps_of.append(jnp.sum(taps0[tap] * pw[0], axis=0, keepdims=True))
    pack_pw.append(grad_pw)
    for l in (1, 2):
        wide = jnp.concatenate([pw[l]] * INN, axis=1)
        grad_pw = jnp.zeros((F, COLS), F32)
        for tap in range(9):
            i, j = tap // 3, tap % 3
            total = jnp.zeros((F, COLS), F32)
            for co in range(OUT):
                at = slice(j * ROWS + co * F, j * ROWS + co * F + F)
                total = total + jnp.where(ci == co + i, acc[l - 1, at, :], 0.0)
            grad_pw = grad_pw + total * repeated(dw[l][tap])
            taps_of.append(fold(jnp.sum(total * wide, axis=0, keepdims=True)))
        pack_pw.append(fold(grad_pw))
    pack_rows = [taps_of[9 * l + tap] for tap in range(9) for l in range(3)]
    for l in range(3):
        pack_rows.append(as_row(jnp.sum(bacc[l], axis=1, keepdims=True))[:, :F])
    pack_rows.append(as_row(jnp.sum(hacc[...], axis=1, keepdims=True))[:, :F])
    pack_rows.append(jnp.zeros((1, F), F32))
    pack_pw.append(jnp.concatenate(pack_rows, axis=0))
    packed = jnp.concatenate(pack_pw, axis=1)
    for k in range(ntm):
        pack[k] = packed[4 * k : 4 * k + 4]

    def scatter(k):
        peer = lax.rem(tm + k, ntm)
        remote(pack.at[peer], r1.at[tm], 3, {"tm": peer}).start()

    each(ntm, scatter)
    r1[tm] = pack[tm]

    def push_out(k):
        peer = lax.rem(me + k, nchan)
        remote(outt.at[rows8(peer), :], got.at[rows8(me), :], 4, {"chan": peer}).start()

    each(nchan, push_out)
    got[rows8(me), :] = outt[rows8(me), :]
    arrived(r1, ntm - 1, 3, tm_peer(1))

    def summed(ref, count):
        total = ref[0]
        for k in range(1, count):
            total = total + ref[k]
        return total

    v1[...] = summed(r1, ntm)
    each(nchan, lambda k: remote(v1, r2.at[me], 5, chan_peer(k)).start())
    r2[me] = v1[...]

    arrived(got, 8 * (nchan - 1), 4, {"chan": right})
    lane = iota((8, 128), 1)
    for k in range(nchan // 2):
        den_out[0, :, 128 * k : 128 * k + 128] = jnp.where(
            lane < OWN, got[16 * k : 16 * k + 8, :], got[16 * k + 8 : 16 * k + 16, :]
        )
    arrived(r2, nchan - 1, 5, {"chan": right})
    v2[...] = summed(r2, nchan)
    each(ntm, lambda k: remote(v2, r3.at[tm], 6, tm_peer(k)).start())
    r3[tm] = v2[...]
    arrived(r3, ntm - 1, 6, tm_peer(1))
    total = jnp.concatenate([r3[k] for k in range(ntm)], axis=0)
    for l in range(3):
        pw_out[l] = total[:, F * l : F * l + F]
    for tap in range(9):
        dw_out[tap] = total[3 * tap : 3 * tap + 3, 3 * F :]
    bias_out[...] = total[27:30, 3 * F :]
    head_out[...] = total[30:31, 3 * F :]


def vmem():
    return pl.BlockSpec(memory_space=pltpu.VMEM)


def on_device(ntm, nchan, recording, blind_mask, dw_kernels, pw_weights, biases, head_weights):
    sds = jax.ShapeDtypeStruct
    scale = SPOT_EVERY / (ntm * nchan * OWN * T)
    dw_grad, pw_grad, bias_grad, head_grad, denoised = pl.pallas_call(
        functools.partial(step, ntm, nchan, scale),
        out_shape=(
            sds((9, 3, F), F32),
            sds((3, F, F), F32),
            sds((3, F), F32),
            sds((1, F), F32),
            sds((1, 8, OWN * nchan), F32),
        ),
        in_specs=[vmem()] * 6,
        out_specs=(vmem(),) * 5,
        scratch_shapes=[
            pltpu.VMEM((80, T), F32),
            pltpu.VMEM((80, T), F32),
            pltpu.VMEM((3, 80, T), F32),
            pltpu.VMEM((8 * F, 144), BF16),
            pltpu.VMEM((2, 3 * ROWS, 3 * COLS), BF16),
            pltpu.VMEM((2, 3 * ROWS, 3 * COLS), BF16),
            pltpu.VMEM((72 * F, T), BF16),
            pltpu.VMEM((72 * F, T), BF16),
            pltpu.VMEM((68 * F, T), BF16),
            pltpu.VMEM((68 * F, T), BF16),
            pltpu.VMEM((72 * F, T), F32),
            pltpu.VMEM((66 * F, T), F32),
            pltpu.VMEM((68 * F, T), BF16),
            pltpu.VMEM((68 * F, T), BF16),
            pltpu.VMEM((74 * F, T), BF16),
            pltpu.VMEM((74 * F, T), BF16),
            pltpu.VMEM((72 * F, T), BF16),
            pltpu.VMEM((72 * F, T), BF16),
            pltpu.VMEM((2, 3 * ROWS, COLS), F32),
            pltpu.VMEM((8 * F, 48), F32),
            pltpu.VMEM((3, F, T), F32),
            pltpu.VMEM((F, T), F32),
            pltpu.VMEM((4, F, T), F32),
            pltpu.VMEM((136, T), F32),
            pltpu.VMEM((T, 128), F32),
            pltpu.VMEM((T, 128), F32),
            pltpu.VMEM((96, T), jnp.int32),
            pltpu.VMEM((T, 128), F32),
            pltpu.VMEM((T, 128), F32),
            pltpu.VMEM((ntm, 4, 128), F32),
            pltpu.VMEM((ntm, 4, 128), F32),
            pltpu.VMEM((4, 128), F32),
            pltpu.VMEM((nchan, 4, 128), F32),
            pltpu.VMEM((4, 128), F32),
            pltpu.VMEM((ntm, 4, 128), F32),
            pltpu.SemaphoreType.DMA((14,)),
        ],
        compiler_params=pltpu.CompilerParams(
            collective_id=0, has_side_effects=True, vmem_limit_bytes=48 << 20
        ),
        name="step",
    )(
        recording,
        blind_mask,
        jnp.transpose(dw_kernels, (2, 0, 1)),
        pw_weights,
        biases,
        head_weights.reshape(1, F),
    )
    return jnp.transpose(dw_grad, (1, 2, 0)), pw_grad, bias_grad, head_grad.reshape(F), denoised


def solution(mesh):
    placed = (P("tm", "chan", None), P("tm", "chan", None), P(), P(), P(), P())
    return jax.shard_map(
        functools.partial(on_device, mesh.shape["tm"], mesh.shape["chan"]),
        mesh=mesh,
        in_specs=placed,
        out_specs=(P(), P(), P(), P(), P("tm", "chan", None)),
        check_vma=False,
    )
```

```python
import functools

import jax
import jax.numpy as jnp
from jax import lax
from jax.experimental import pallas as pl
from jax.experimental.pallas import tpu as pltpu
from jax.sharding import PartitionSpec as P

SPOT_EVERY = 8
F = 32
T = 256
OWN = 64
HALO = 3
OUT = 6
INN = 8
ROWS = OUT * F
COLS = INN * F
NBLK = 11
MESH = pl.DeviceIdType.MESH
F32 = jnp.float32
BF16 = jnp.bfloat16


def aligned(start, size):
    return start if isinstance(start, int) else pl.multiple_of(start, size)


def run(count, body):
    for b in range(count):
        body(b)


def iota(shape, dim):
    return lax.broadcasted_iota(jnp.int32, shape, dim)


def split(x):
    hi = x.astype(BF16)
    return hi, (x - hi.astype(F32)).astype(BF16)


def later(x):
    first = iota((x.shape[0], 128), 1) == 0
    a, b = pltpu.roll(x[:, :128], 1, 1), pltpu.roll(x[:, 128:], 1, 1)
    return jnp.concatenate([jnp.where(first, 0.0, a), jnp.where(first, a, b)], axis=1)


def earlier(x):
    last = iota((x.shape[0], 128), 1) == 127
    a, b = pltpu.roll(x[:, :128], 127, 1), pltpu.roll(x[:, 128:], 127, 1)
    return jnp.concatenate([jnp.where(last, b, a), jnp.where(last, 0.0, b)], axis=1)


def dot(a, b):
    return jnp.dot(a, b, preferred_element_type=F32)


def dot_t(a, b):
    return lax.dot_general(a, b, (((1,), (1,)), ((), ())), preferred_element_type=F32)


def repeated(row):
    return jnp.concatenate([row] * INN, axis=1)


def as_column(row):
    return jnp.sum(jnp.where(iota((F, F), 0) == iota((F, F), 1), row, 0.0), axis=1, keepdims=True)


def as_row(column):
    same = iota((F, COLS), 0) == (iota((F, COLS), 1) & (F - 1))
    return jnp.sum(jnp.where(same, column, 0.0), axis=0, keepdims=True)


def fill_windows(rec_ref, send):
    lane = iota((8, 128), 1)
    tiles = rec_ref.shape[2] // 128
    zero = jnp.zeros((8, 128), F32)
    tile = [rec_ref[0, :, 128 * k : 128 * k + 128] for k in range(tiles)]
    for k in range(tiles):
        before = tile[k - 1] if k > 0 else zero
        after = tile[k + 1] if k < tiles - 1 else zero
        even = jnp.where(lane < HALO, pltpu.roll(before, HALO, 1), pltpu.roll(tile[k], HALO, 1))
        odd = jnp.where(
            lane < OWN + HALO,
            pltpu.roll(tile[k], OWN + HALO, 1),
            pltpu.roll(after, OWN + HALO, 1),
        )
        send[16 * k : 16 * k + 8, :] = even
        send[16 * k + 8 : 16 * k + 16, :] = odd


def forward_weights(lhs, pw, dw):
    wide = jnp.concatenate([pw] * INN, axis=1)
    ci = iota((F, COLS), 1) >> 5
    rows = [repeated(row) for row in dw]
    for j in range(3):
        for co in range(OUT):
            taps = jnp.zeros((F, COLS), F32)
            for i in range(3):
                taps = jnp.where(ci == co + i, rows[3 * i + j], taps)
            hi, lo = split(wide * taps)
            at = slice(j * ROWS + co * F, j * ROWS + co * F + F)
            lhs[at, 0:COLS] = hi
            lhs[at, COLS : 2 * COLS] = lo
            lhs[at, 2 * COLS : 3 * COLS] = hi


def backward_weights(lhs, pw_t, dw):
    wide = jnp.concatenate([pw_t] * INN, axis=1)
    ci = iota((F, COLS), 1) >> 5
    cols = [jnp.broadcast_to(as_column(row), (F, COLS)) for row in dw]
    for j in range(3):
        for co in range(OUT):
            taps = jnp.zeros((F, COLS), F32)
            for i in range(3):
                taps = jnp.where(ci == co + 2 - i, cols[3 * i + j], taps)
            hi, lo = split(wide * taps)
            at = slice(j * ROWS + co * F, j * ROWS + co * F + F)
            lhs[at, 0:COLS] = hi
            lhs[at, COLS : 2 * COLS] = lo
            lhs[at, 2 * COLS : 3 * COLS] = hi


def first_weights(lhs, pw, dw):
    lane = iota((F, 144), 1)
    part = (lane >= 48).astype(jnp.int32) + (lane >= 96).astype(jnp.int32)
    spot = lane - 48 * part
    j_of, ci = spot >> 4, spot & 15
    cols = [jnp.sum(pw * row, axis=1, keepdims=True) for row in dw]
    for co in range(8):
        taps = jnp.zeros((F, 144), F32)
        for tap in range(9):
            here = (ci == co + tap // 3) & (j_of == tap % 3)
            taps = jnp.where(here, cols[tap], taps)
        hi = taps.astype(BF16).astype(F32)
        lhs[co * F : co * F + F, :] = jnp.where(part == 1, taps - hi, hi).astype(BF16)


def tripled(hi, lo):
    return jnp.concatenate([hi, hi, lo], axis=0)


def silu_parts(pre):
    s = 0.5 * jnp.tanh(0.5 * pre) + 0.5
    a = pre * s
    return a, s + (a - a * s)


def mixed(lhs, hi, lo, flip):
    prod = dot(lhs[...], tripled(hi, lo))
    first, mid, last = prod[:ROWS], prod[ROWS : 2 * ROWS], prod[2 * ROWS :]
    if flip:
        first, last = last, first
    return mid + later(first) + earlier(last)


def fold(x):
    y = x[:, :128] + x[:, 128:]
    y = y + pltpu.roll(y, 64, 1)
    y = y + pltpu.roll(y, 32, 1)
    return y[:, :F]


def shifted_triple(g):
    hi, lo = split(g)
    parts = []
    for move in (earlier, lambda x: x, later):
        a, b = move(hi), move(lo)
        parts.append(jnp.concatenate([a, b, a], axis=1))
    return jnp.concatenate(parts, axis=0)


def add_channels(acc, g):
    total = acc[...]
    for k in range(OUT):
        total = total + g[k * F : k * F + F]
    acc[...] = total


def step(
    ntm, nchan, scale,
    rec_hbm, mask_hbm, dw_hbm, pw_hbm, bias_hbm, head_hbm, den_out, total_out,
    sig, coef, wins, lhs0, lhs_f, lhs_b, a1h, a1l, a2h, a2l, d0, d1,
    g2h, g2l, g1h, g1l, g0h, g0l, acc, acc0, bacc, hacc, bcol, outs,
    rec_ref, dw_ref, pw_ref, bias_ref, head_ref, lsems, send, win, maskx, outt, got,
    pack, ra, va, rb, vb, rc, pack0, r0a, v0, r0b, sems,
):
    me, tm = lax.axis_index("chan"), lax.axis_index("tm")
    right, left = lax.rem(me + 1, nchan), lax.rem(me + nchan - 1, nchan)
    barrier = pltpu.get_barrier_semaphore()

    def chan_peer(k):
        return {"chan": lax.rem(me + k, nchan)}

    def tm_peer(k):
        return {"tm": lax.rem(tm + k, ntm)}

    def each(count, go):
        def body(k, carry):
            go(k)
            return carry

        lax.fori_loop(1, count, body, 0)

    def greet(where):
        pl.semaphore_signal(barrier, inc=1, device_id=where, device_id_type=MESH)

    def remote(src, dst, pair, where):
        return pltpu.make_async_remote_copy(
            src_ref=src,
            dst_ref=dst,
            send_sem=sems.at[2 * pair],
            recv_sem=sems.at[2 * pair + 1],
            device_id=where,
            device_id_type=MESH,
        )

    def rows8(index):
        return pl.ds(pl.multiple_of(index * 8, 8), 8)

    def arrived(dst, count, pair, where):
        remote(dst.at[pl.ds(0, count)], dst.at[pl.ds(0, count)], pair, where).wait()

    own_rows = pl.ds(8, OWN)
    loads = [
        pltpu.make_async_copy(src, dst, lsems.at[k])
        for k, (src, dst) in enumerate(
            (
                (rec_hbm, rec_ref),
                (mask_hbm.at[0], maskx.at[own_rows, :]),
                (dw_hbm, dw_ref),
                (pw_hbm, pw_ref),
                (bias_hbm, bias_ref),
                (head_hbm, head_ref),
            )
        )
    ]
    for load in loads:
        load.start()
    each(nchan, lambda k: greet(chan_peer(k)))
    each(ntm, lambda k: greet(tm_peer(k)))
    loads[0].wait()
    fill_windows(rec_ref, send)
    for load in loads[1:]:
        load.wait()
    pl.semaphore_wait(barrier, nchan - 1 + ntm - 1)

    to_right = remote(
        maskx.at[pl.ds(OWN, 8), :], maskx.at[pl.ds(0, 8), :], 0, {"chan": right}
    )
    to_left = remote(
        maskx.at[pl.ds(8, 8), :], maskx.at[pl.ds(OWN + 8, 8), :], 1, {"chan": left}
    )

    def push_in(k):
        peer = lax.rem(me + k, nchan)
        remote(send.at[rows8(peer), :], win.at[rows8(me), :], 2, {"chan": peer}).start()

    each(nchan, push_in)
    to_right.start()
    to_left.start()
    win[rows8(me), :] = send[rows8(me), :]
    maskx[OWN + 16 :, :] = jnp.zeros((16, T), jnp.int32)

    dw = [[dw_ref[tap, l : l + 1, :] for tap in range(9)] for l in range(3)]
    pw = [pw_ref[l] for l in range(3)]
    first_weights(lhs0, pw[0], dw[0])
    for l in (1, 2):
        forward_weights(lhs_f.at[l - 1], pw[l], dw[l])
        backward_weights(lhs_b.at[l - 1], pw[l].T, dw[l])
    for l in range(3):
        bcol[l] = jnp.broadcast_to(as_column(bias_ref[l : l + 1, :]), (F, T))
    bcol[3] = jnp.broadcast_to(as_column(head_ref[...]), (F, T))

    zero2 = jnp.zeros((2 * F, T), BF16)
    for ref in (g2h, g2l, g1h, g1l):
        ref[: 2 * F, :] = zero2
    for ref in (g1h, g1l):
        ref[68 * F :, :] = jnp.zeros((6 * F, T), BF16)
    for ref in (a2h, a2l):
        ref[66 * F :, :] = zero2
    acc[...] = jnp.zeros_like(acc)
    acc0[...] = jnp.zeros_like(acc0)
    bacc[...] = jnp.zeros_like(bacc)
    hacc[...] = jnp.zeros_like(hacc)
    outs[...] = jnp.zeros_like(outs)

    to_right.wait()
    to_left.wait()
    arrived(win, 8 * (nchan - 1), 2, {"chan": right})
    turned = win[...].T
    sig[...] = turned[:80]
    blind = maskx[5:85, :] == 1
    coef[...] = jnp.where(blind, 2.0 * scale, 0.0)
    act0 = jnp.where(blind, 0.0, turned[:80])
    wins[0] = later(act0)
    wins[1] = act0
    wins[2] = earlier(act0)

    def columns(b):
        return [split(wins[j, pl.ds(aligned(8 * b, 8), 16), :]) for j in range(3)]

    def layer0(b):
        parts = columns(b)
        hi = jnp.concatenate([p[0] for p in parts], axis=0)
        lo = jnp.concatenate([p[1] for p in parts], axis=0)
        pre = dot(lhs0[...], tripled(hi, lo))
        pre = pre + jnp.concatenate([bcol[0]] * 8, axis=0)
        a, d = silu_parts(pre)
        at = pl.ds(aligned(b * 8 * F, F), 8 * F)
        a1h[at, :], a1l[at, :] = split(a)
        d0[at, :] = d

    run(9, layer0)

    def clear(ends, refs):
        for ref in refs:
            ref[ends, :] = jnp.zeros(((ends.stop - ends.start), T), ref.dtype)

    @pl.when(me == 0)
    def _():
        clear(slice(0, 2 * F), (a1h, a1l, d0))

    @pl.when(me == nchan - 1)
    def _():
        clear(slice(66 * F, 68 * F), (a1h, a1l, d0))

    def inputs(b):
        return pl.ds(aligned(b * ROWS, F), COLS)

    def outputs(b, ahead=0):
        return pl.ds(aligned(b * ROWS + ahead * F, F), ROWS)

    def layer1(b):
        pre = mixed(lhs_f.at[0], a1h[inputs(b), :], a1l[inputs(b), :], False)
        pre = pre + jnp.concatenate([bcol[1]] * OUT, axis=0)
        a, d = silu_parts(pre)
        a2h[outputs(b), :], a2l[outputs(b), :] = split(a)
        d1[outputs(b), :] = d

    run(NBLK, layer1)

    @pl.when(me == 0)
    def _():
        clear(slice(0, F), (a2h, a2l, d1))

    @pl.when(me == nchan - 1)
    def _():
        clear(slice(65 * F, 66 * F), (a2h, a2l, d1))

    par = lax.rem(me, 2) * OWN

    def layer2(b):
        ah, al = a2h[inputs(b), :], a2l[inputs(b), :]
        pre = mixed(lhs_f.at[1], ah, al, False)
        pre = pre + jnp.concatenate([bcol[2]] * OUT, axis=0)
        a, d = silu_parts(pre)
        head = bcol[3]
        heads = hacc[...]
        grads = []
        for k in range(OUT):
            at = slice(k * F, k * F + F)
            row = jnp.sum(head * a[at], axis=0, keepdims=True)
            outs[pl.ds(par + OUT * b + k, 1), :] = row
            spot = pl.ds(OUT * b + k + HALO, 1)
            g_out = jnp.where(OUT * b + k < OWN, coef[spot, :], 0.0) * (row - sig[spot, :])
            heads = heads + g_out * a[at]
            grads.append((head * d[at]) * g_out)
        hacc[...] = heads
        g = jnp.concatenate(grads, axis=0)
        g2h[outputs(b, 2), :], g2l[outputs(b, 2), :] = split(g)
        add_channels(bacc.at[2], g)
        acc[1] += dot_t(shifted_triple(g), jnp.concatenate([ah, ah, al], axis=1))

    run(NBLK, layer2)

    outt[...] = outs[:128, :].T

    def back2(b):
        g_act = mixed(lhs_b.at[1], g2h[inputs(b), :], g2l[inputs(b), :], True)
        g = g_act * d1[outputs(b), :]
        g1h[outputs(b, 2), :], g1l[outputs(b, 2), :] = split(g)
        add_channels(bacc.at[1], g)
        ah, al = a1h[inputs(b), :], a1l[inputs(b), :]
        acc[0] += dot_t(shifted_triple(g), jnp.concatenate([ah, ah, al], axis=1))

    def push_out(k):
        peer = lax.rem(me + k, nchan)
        remote(outt.at[rows8(peer), :], got.at[rows8(me), :], 4, {"chan": peer}).start()

    run(NBLK, back2)

    ci = iota((F, COLS), 1) >> 5
    rows_of, pack_pw = {}, []
    for l in (1, 2):
        wide = jnp.concatenate([pw[l]] * INN, axis=1)
        grad_pw = jnp.zeros((F, COLS), F32)
        for tap in range(9):
            i, j = tap // 3, tap % 3
            total = jnp.zeros((F, COLS), F32)
            for co in range(OUT):
                at = slice(j * ROWS + co * F, j * ROWS + co * F + F)
                total = total + jnp.where(ci == co + i, acc[l - 1, at, :], 0.0)
            grad_pw = grad_pw + total * repeated(dw[l][tap])
            rows_of[l, tap] = fold(jnp.sum(total * wide, axis=0, keepdims=True))
        pack_pw.append(fold(grad_pw))
    pack_rows = [rows_of[l, tap] for tap in range(9) for l in (1, 2)]
    for sums in (bacc[1], bacc[2], hacc[...]):
        pack_rows.append(as_row(jnp.sum(sums, axis=1, keepdims=True))[:, :F])
    pack_rows.append(jnp.zeros((F - 21, F), F32))
    pack_pw.append(jnp.concatenate(pack_rows, axis=0))
    pack_pw.append(jnp.zeros((F, F), F32))
    pack[...] = jnp.concatenate(pack_pw, axis=1)

    def summed(ref, count):
        total = ref[0]
        for k in range(1, count):
            total = total + ref[k]
        return total

    near = 8
    far = nchan // near
    base = (me // near) * near

    def near_peer(k):
        return {"chan": base + lax.rem(me - base + k, near)}

    def far_peer(k):
        return {"chan": lax.rem(me + near * k, nchan)}

    def back1(b):
        g_act = mixed(lhs_b.at[0], g1h[inputs(b), :], g1l[inputs(b), :], True)
        g = g_act * d0[outputs(b), :]
        g0h[outputs(b), :], g0l[outputs(b), :] = split(g)
        add_channels(bacc.at[0], g)

    each(ntm, lambda k: remote(pack, ra.at[tm], 3, tm_peer(k)).start())
    ra[tm] = pack[...]
    run(NBLK + 1, back1)

    def grads0(b):
        parts = columns(b)
        hi = jnp.concatenate([p[0] for p in parts], axis=0)
        lo = jnp.concatenate([p[1] for p in parts], axis=0)
        at = pl.ds(aligned(b * 8 * F, F), 8 * F)
        gh, gl = g0h[at, :], g0l[at, :]
        left = jnp.concatenate([gh, gl, gh], axis=1)
        right = jnp.concatenate([hi, hi, lo], axis=1)
        acc0[...] += dot_t(left, right)

    run(9, grads0)

    lane48 = iota((F, 48), 1)
    firsts = []
    for tap in range(9):
        total = jnp.zeros((F, 48), F32)
        for co in range(8):
            here = lane48 == (tap % 3) * 16 + co + tap // 3
            total = total + jnp.where(here, acc0[co * F : co * F + F, :], 0.0)
        firsts.append(as_row(jnp.sum(total, axis=1, keepdims=True))[:, :128])
    firsts.append(as_row(jnp.sum(bacc[0], axis=1, keepdims=True))[:, :128])
    group = iota((1, 128), 1) >> 5
    for r in range(3):
        row = jnp.zeros((1, 128), F32)
        for q, first in enumerate(firsts[4 * r : 4 * r + 4]):
            row = jnp.where(group == q, first, row)
        pack0[r : r + 1, :] = row
    pack0[3:4, :] = jnp.zeros((1, 128), F32)
    each(ntm, lambda k: remote(pack0, r0a.at[tm], 7, tm_peer(k)).start())
    r0a[tm] = pack0[...]

    each(nchan, push_out)
    got[rows8(me), :] = outt[rows8(me), :]
    arrived(ra, ntm - 1, 3, tm_peer(1))
    va[...] = summed(ra, ntm)
    each(near, lambda k: remote(va, rb.at[me - base], 5, near_peer(k)).start())
    rb[me - base] = va[...]

    arrived(r0a, ntm - 1, 7, tm_peer(1))
    v0[...] = summed(r0a, ntm)
    each(nchan, lambda k: remote(v0, r0b.at[me], 8, chan_peer(k)).start())
    r0b[me] = v0[...]

    arrived(rb, near - 1, 5, near_peer(1))
    vb[...] = summed(rb, near)
    each(far, lambda k: remote(vb, rc.at[me // near], 6, far_peer(k)).start())
    rc[me // near] = vb[...]

    arrived(got, 8 * (nchan - 1), 4, {"chan": right})
    lane = iota((8, 128), 1)
    for k in range(nchan // 2):
        den_out[:, 128 * k : 128 * k + 128] = jnp.where(
            lane < OWN, got[16 * k : 16 * k + 8, :], got[16 * k + 8 : 16 * k + 16, :]
        )
    arrived(r0b, nchan - 1, 8, {"chan": right})
    sums = summed(r0b, nchan)
    rows = [sums[k // 4 : k // 4 + 1, F * (k % 4) : F * (k % 4) + F] for k in range(10)]
    grad_pw = jnp.zeros((F, F), F32)
    final_rows = []
    for tap in range(9):
        column = as_column(rows[tap])
        grad_pw = grad_pw + column * dw[0][tap]
        final_rows.append(jnp.sum(column * pw[0], axis=0, keepdims=True))
    final_rows.append(rows[9])
    final_rows.append(jnp.zeros((1, F), F32))
    arrived(rc, far - 1, 6, far_peer(1))
    later_layers = summed(rc, far)
    all_rows = jnp.concatenate([later_layers[:21, 2 * F : 3 * F]] + final_rows, axis=0)
    total_out[...] = jnp.concatenate([later_layers[:, : 2 * F], all_rows, grad_pw], axis=1)


def unpack(den_ref, total_ref, dw_out, pw_out, bias_out, head_out, den_out):
    den_out[0] = den_ref[...]
    total = total_ref[...]
    pw_out[0] = total[:, 3 * F :]
    pw_out[1] = total[:, :F]
    pw_out[2] = total[:, F : 2 * F]
    rows = total[:, 2 * F : 3 * F]
    for tap in range(9):
        dw_out[tap, 0:1, :] = rows[21 + tap : 22 + tap]
        dw_out[tap, 1:3, :] = rows[2 * tap : 2 * tap + 2]
    bias_out[0:1, :] = rows[30:31]
    bias_out[1:3, :] = rows[18:20]
    head_out[...] = rows[20:21]


def vmem():
    return pl.BlockSpec(memory_space=pltpu.VMEM)


def on_device(ntm, nchan, recording, blind_mask, dw_kernels, pw_weights, biases, head_weights):
    sds = jax.ShapeDtypeStruct
    scale = SPOT_EVERY / (ntm * nchan * OWN * T)
    den, total = pl.pallas_call(
        functools.partial(step, ntm, nchan, scale),
        out_shape=(sds((8, OWN * nchan), F32), sds((F, 128), F32)),
        in_specs=[pl.BlockSpec(memory_space=pltpu.HBM)] * 6,
        out_specs=(vmem(),) * 2,
        scratch_shapes=[
            pltpu.VMEM((80, T), F32),
            pltpu.VMEM((80, T), F32),
            pltpu.VMEM((3, 80, T), F32),
            pltpu.VMEM((8 * F, 144), BF16),
            pltpu.VMEM((2, 3 * ROWS, 3 * COLS), BF16),
            pltpu.VMEM((2, 3 * ROWS, 3 * COLS), BF16),
            pltpu.VMEM((72 * F, T), BF16),
            pltpu.VMEM((72 * F, T), BF16),
            pltpu.VMEM((68 * F, T), BF16),
            pltpu.VMEM((68 * F, T), BF16),
            pltpu.VMEM((72 * F, T), F32),
            pltpu.VMEM((66 * F, T), F32),
            pltpu.VMEM((68 * F, T), BF16),
            pltpu.VMEM((68 * F, T), BF16),
            pltpu.VMEM((74 * F, T), BF16),
            pltpu.VMEM((74 * F, T), BF16),
            pltpu.VMEM((72 * F, T), BF16),
            pltpu.VMEM((72 * F, T), BF16),
            pltpu.VMEM((2, 3 * ROWS, COLS), F32),
            pltpu.VMEM((8 * F, 48), F32),
            pltpu.VMEM((3, F, T), F32),
            pltpu.VMEM((F, T), F32),
            pltpu.VMEM((4, F, T), F32),
            pltpu.VMEM((136, T), F32),
            pltpu.VMEM((1, 8, OWN * nchan), F32),
            pltpu.VMEM((9, 3, F), F32),
            pltpu.VMEM((3, F, F), F32),
            pltpu.VMEM((3, F), F32),
            pltpu.VMEM((1, F), F32),
            pltpu.SemaphoreType.DMA((6,)),
            pltpu.VMEM((T, 128), F32),
            pltpu.VMEM((T, 128), F32),
            pltpu.VMEM((96, T), jnp.int32),
            pltpu.VMEM((T, 128), F32),
            pltpu.VMEM((T, 128), F32),
            pltpu.VMEM((F, 128), F32),
            pltpu.VMEM((ntm, F, 128), F32),
            pltpu.VMEM((F, 128), F32),
            pltpu.VMEM((8, F, 128), F32),
            pltpu.VMEM((F, 128), F32),
            pltpu.VMEM((nchan // 8, F, 128), F32),
            pltpu.VMEM((4, 128), F32),
            pltpu.VMEM((ntm, 4, 128), F32),
            pltpu.VMEM((4, 128), F32),
            pltpu.VMEM((nchan, 4, 128), F32),
            pltpu.SemaphoreType.DMA((18,)),
        ],
        compiler_params=pltpu.CompilerParams(
            collective_id=0, has_side_effects=True, vmem_limit_bytes=62 << 20
        ),
        name="step",
    )(
        recording,
        blind_mask,
        jnp.transpose(dw_kernels, (2, 0, 1)),
        pw_weights,
        biases,
        head_weights.reshape(1, F),
    )
    dw_grad, pw_grad, bias_grad, head_grad, denoised = pl.pallas_call(
        unpack,
        out_shape=(
            sds((9, 3, F), F32),
            sds((3, F, F), F32),
            sds((3, F), F32),
            sds((1, F), F32),
            sds((1, 8, OWN * nchan), F32),
        ),
        in_specs=[vmem()] * 2,
        out_specs=(vmem(),) * 5,
        compiler_params=pltpu.CompilerParams(vmem_limit_bytes=62 << 20),
        name="unpack",
    )(den, total)
    return jnp.transpose(dw_grad, (1, 2, 0)), pw_grad, bias_grad, head_grad.reshape(F), denoised


def solution(mesh):
    placed = (P("tm", "chan", None), P("tm", "chan", None), P(), P(), P(), P())
    return jax.shard_map(
        functools.partial(on_device, mesh.shape["tm"], mesh.shape["chan"]),
        mesh=mesh,
        in_specs=placed,
        out_specs=(P(), P(), P(), P(), P("tm", "chan", None)),
        check_vma=False,
    )
```

```python
import functools

import jax
import jax.numpy as jnp
from jax import lax
from jax.experimental import pallas as pl
from jax.experimental.pallas import tpu as pltpu
from jax.sharding import PartitionSpec as P

SPOT_EVERY = 8
F = 32
T = 256
OWN = 64
HALO = 3
OUT = 6
INN = 8
ROWS = OUT * F
COLS = INN * F
NBLK = 11
MESH = pl.DeviceIdType.MESH
F32 = jnp.float32
BF16 = jnp.bfloat16


def aligned(start, size):
    return start if isinstance(start, int) else pl.multiple_of(start, size)


def run(count, body):
    for b in range(count):
        body(b)


def without(x, start, stop, outside):
    parts = [x[: start * F]] if start else []
    parts.append(jnp.where(outside, 0.0, x[start * F : stop * F]))
    if stop * F < x.shape[0]:
        parts.append(x[stop * F :])
    return jnp.concatenate(parts, axis=0)


def iota(shape, dim):
    return lax.broadcasted_iota(jnp.int32, shape, dim)


def split(x):
    hi = x.astype(BF16)
    return hi, (x - hi.astype(F32)).astype(BF16)


def later(x):
    first = iota((x.shape[0], 128), 1) == 0
    a, b = pltpu.roll(x[:, :128], 1, 1), pltpu.roll(x[:, 128:], 1, 1)
    return jnp.concatenate([jnp.where(first, 0.0, a), jnp.where(first, a, b)], axis=1)


def earlier(x):
    last = iota((x.shape[0], 128), 1) == 127
    a, b = pltpu.roll(x[:, :128], 127, 1), pltpu.roll(x[:, 128:], 127, 1)
    return jnp.concatenate([jnp.where(last, b, a), jnp.where(last, 0.0, b)], axis=1)


def dot(a, b):
    return jnp.dot(a, b, preferred_element_type=F32)


def dot_t(a, b):
    return lax.dot_general(a, b, (((1,), (1,)), ((), ())), preferred_element_type=F32)


def repeated(row):
    return jnp.concatenate([row] * INN, axis=1)


def as_column(row):
    return jnp.sum(jnp.where(iota((F, F), 0) == iota((F, F), 1), row, 0.0), axis=1, keepdims=True)


def as_row(column):
    same = iota((F, COLS), 0) == (iota((F, COLS), 1) & (F - 1))
    return jnp.sum(jnp.where(same, column, 0.0), axis=0, keepdims=True)


def fill_windows(rec_ref, send):
    lane = iota((8, 128), 1)
    tiles = rec_ref.shape[2] // 128
    zero = jnp.zeros((8, 128), F32)
    tile = [rec_ref[0, :, 128 * k : 128 * k + 128] for k in range(tiles)]
    for k in range(tiles):
        before = tile[k - 1] if k > 0 else zero
        after = tile[k + 1] if k < tiles - 1 else zero
        even = jnp.where(lane < HALO, pltpu.roll(before, HALO, 1), pltpu.roll(tile[k], HALO, 1))
        odd = jnp.where(
            lane < OWN + HALO,
            pltpu.roll(tile[k], OWN + HALO, 1),
            pltpu.roll(after, OWN + HALO, 1),
        )
        send[16 * k : 16 * k + 8, :] = even
        send[16 * k + 8 : 16 * k + 16, :] = odd


def forward_weights(lhs, pw, dw):
    wide = jnp.concatenate([pw] * INN, axis=1)
    ci = iota((F, COLS), 1) >> 5
    rows = [repeated(row) for row in dw]
    for j in range(3):
        for co in range(OUT):
            taps = jnp.zeros((F, COLS), F32)
            for i in range(3):
                taps = jnp.where(ci == co + i, rows[3 * i + j], taps)
            hi, lo = split(wide * taps)
            at = slice(j * ROWS + co * F, j * ROWS + co * F + F)
            lhs[at, 0:COLS] = hi
            lhs[at, COLS : 2 * COLS] = lo
            lhs[at, 2 * COLS : 3 * COLS] = hi


def backward_weights(lhs, pw_t, dw):
    wide = jnp.concatenate([pw_t] * INN, axis=1)
    ci = iota((F, COLS), 1) >> 5
    cols = [jnp.broadcast_to(as_column(row), (F, COLS)) for row in dw]
    for j in range(3):
        for co in range(OUT):
            taps = jnp.zeros((F, COLS), F32)
            for i in range(3):
                taps = jnp.where(ci == co + 2 - i, cols[3 * i + j], taps)
            hi, lo = split(wide * taps)
            at = slice(j * ROWS + co * F, j * ROWS + co * F + F)
            lhs[at, 0:COLS] = hi
            lhs[at, COLS : 2 * COLS] = lo
            lhs[at, 2 * COLS : 3 * COLS] = hi


def first_weights(lhs, pw, dw):
    lane = iota((F, 144), 1)
    part = (lane >= 48).astype(jnp.int32) + (lane >= 96).astype(jnp.int32)
    spot = lane - 48 * part
    j_of, ci = spot >> 4, spot & 15
    cols = [jnp.sum(pw * row, axis=1, keepdims=True) for row in dw]
    for co in range(8):
        taps = jnp.zeros((F, 144), F32)
        for tap in range(9):
            here = (ci == co + tap // 3) & (j_of == tap % 3)
            taps = jnp.where(here, cols[tap], taps)
        hi = taps.astype(BF16).astype(F32)
        lhs[co * F : co * F + F, :] = jnp.where(part == 1, taps - hi, hi).astype(BF16)


def tripled(hi, lo):
    return jnp.concatenate([hi, hi, lo], axis=0)


def silu_parts(pre):
    s = 0.5 * jnp.tanh(0.5 * pre) + 0.5
    a = pre * s
    return a, s + (a - a * s)


def mixed(lhs, hi, lo, flip):
    prod = dot(lhs[...], tripled(hi, lo))
    first, mid, last = prod[:ROWS], prod[ROWS : 2 * ROWS], prod[2 * ROWS :]
    if flip:
        first, last = last, first
    return mid + later(first) + earlier(last)


def fold(x):
    y = x[:, :128] + x[:, 128:]
    y = y + pltpu.roll(y, 64, 1)
    y = y + pltpu.roll(y, 32, 1)
    return y[:, :F]


def shifted_triple(g):
    hi, lo = split(g)
    parts = []
    for move in (earlier, lambda x: x, later):
        a, b = move(hi), move(lo)
        parts.append(jnp.concatenate([a, b, a], axis=1))
    return jnp.concatenate(parts, axis=0)


def add_channels(acc, g):
    total = acc[...]
    for k in range(OUT):
        total = total + g[k * F : k * F + F]
    acc[...] = total


def step(
    ntm, nchan, scale,
    rec_hbm, mask_hbm, dw_hbm, pw_hbm, bias_hbm, head_hbm, den_out, total_out,
    sig, coef, wins, lhs0, lhs_f, lhs_b, a1h, a1l, a2h, a2l, d0, d1,
    g2h, g2l, g1h, g1l, g0h, g0l, acc, acc0, bacc, hacc, bcol, outs,
    rec_ref, dw_ref, pw_ref, bias_ref, head_ref, lsems, send, win, maskx, outt, got,
    pack, ra, va, rb, vb, rc, pack0, r0a, v0, r0b, sems,
):
    me, tm = lax.axis_index("chan"), lax.axis_index("tm")
    right, left = lax.rem(me + 1, nchan), lax.rem(me + nchan - 1, nchan)
    barrier = pltpu.get_barrier_semaphore()

    def chan_peer(k):
        return {"chan": lax.rem(me + k, nchan)}

    def tm_peer(k):
        return {"tm": lax.rem(tm + k, ntm)}

    def each(count, go):
        def body(k, carry):
            go(k)
            return carry

        lax.fori_loop(1, count, body, 0)

    def each_chan(go):
        others = nchan - 8

        def body(k, carry):
            go(8 + lax.rem(k + 8, others))
            return carry

        lax.fori_loop(0, others, body, 0)
        each(8, go)

    def greet(where):
        pl.semaphore_signal(barrier, inc=1, device_id=where, device_id_type=MESH)

    def remote(src, dst, pair, where):
        return pltpu.make_async_remote_copy(
            src_ref=src,
            dst_ref=dst,
            send_sem=sems.at[2 * pair],
            recv_sem=sems.at[2 * pair + 1],
            device_id=where,
            device_id_type=MESH,
        )

    def rows8(index):
        return pl.ds(pl.multiple_of(index * 8, 8), 8)

    def arrived(dst, count, pair, where):
        remote(dst.at[pl.ds(0, count)], dst.at[pl.ds(0, count)], pair, where).wait()

    own_rows = pl.ds(8, OWN)
    loads = [
        pltpu.make_async_copy(src, dst, lsems.at[k])
        for k, (src, dst) in enumerate(
            (
                (rec_hbm, rec_ref),
                (mask_hbm.at[0], maskx.at[own_rows, :]),
                (dw_hbm, dw_ref),
                (pw_hbm, pw_ref),
                (bias_hbm, bias_ref),
                (head_hbm, head_ref),
            )
        )
    ]
    for load in loads:
        load.start()
    each_chan(lambda k: greet(chan_peer(k)))
    each(ntm, lambda k: greet(tm_peer(k)))
    loads[0].wait()
    fill_windows(rec_ref, send)
    for load in loads[1:]:
        load.wait()
    pl.semaphore_wait(barrier, nchan - 1 + ntm - 1)

    to_right = remote(
        maskx.at[pl.ds(OWN, 8), :], maskx.at[pl.ds(0, 8), :], 0, {"chan": right}
    )
    to_left = remote(
        maskx.at[pl.ds(8, 8), :], maskx.at[pl.ds(OWN + 8, 8), :], 1, {"chan": left}
    )

    def push_in(k):
        peer = lax.rem(me + k, nchan)
        remote(send.at[rows8(peer), :], win.at[rows8(me), :], 2, {"chan": peer}).start()

    each_chan(push_in)
    to_right.start()
    to_left.start()
    win[rows8(me), :] = send[rows8(me), :]
    maskx[OWN + 16 :, :] = jnp.zeros((16, T), jnp.int32)

    dw = [[dw_ref[tap, l : l + 1, :] for tap in range(9)] for l in range(3)]
    pw = [pw_ref[l] for l in range(3)]
    first_weights(lhs0, pw[0], dw[0])
    for l in (1, 2):
        forward_weights(lhs_f.at[l - 1], pw[l], dw[l])
        backward_weights(lhs_b.at[l - 1], pw[l].T, dw[l])
    for l in range(3):
        bcol[l] = jnp.broadcast_to(as_column(bias_ref[l : l + 1, :]), (F, T))
    bcol[3] = jnp.broadcast_to(as_column(head_ref[...]), (F, T))

    zero2 = jnp.zeros((2 * F, T), BF16)
    for ref in (g2h, g2l, g1h, g1l):
        ref[: 2 * F, :] = zero2
    for ref in (g1h, g1l):
        ref[68 * F :, :] = jnp.zeros((6 * F, T), BF16)
    for ref in (a2h, a2l):
        ref[66 * F :, :] = zero2
    acc[...] = jnp.zeros_like(acc)
    acc0[...] = jnp.zeros_like(acc0)
    bacc[...] = jnp.zeros_like(bacc)
    hacc[...] = jnp.zeros_like(hacc)
    outs[...] = jnp.zeros_like(outs)

    to_right.wait()
    to_left.wait()
    arrived(win, 8 * (nchan - 1), 2, {"chan": right})
    turned = win[...].T
    sig[...] = turned[:80]
    blind = maskx[5:85, :] == 1
    coef[...] = jnp.where(blind, 2.0 * scale, 0.0)
    act0 = jnp.where(blind, 0.0, turned[:80])
    wins[0] = later(act0)
    wins[1] = act0
    wins[2] = earlier(act0)

    def columns(b):
        return [split(wins[j, pl.ds(aligned(8 * b, 8), 16), :]) for j in range(3)]

    def layer0(b):
        parts = columns(b)
        hi = jnp.concatenate([p[0] for p in parts], axis=0)
        lo = jnp.concatenate([p[1] for p in parts], axis=0)
        pre = dot(lhs0[...], tripled(hi, lo))
        pre = pre + jnp.concatenate([bcol[0]] * 8, axis=0)
        a, d = silu_parts(pre)
        if b == 0:
            a, d = (without(x, 0, 2, me == 0) for x in (a, d))
        if b == 8:
            a, d = (without(x, 2, 4, me == nchan - 1) for x in (a, d))
        at = pl.ds(aligned(b * 8 * F, F), 8 * F)
        a1h[at, :], a1l[at, :] = split(a)
        d0[at, :] = d

    run(9, layer0)

    def inputs(b):
        return pl.ds(aligned(b * ROWS, F), COLS)

    def outputs(b, ahead=0):
        return pl.ds(aligned(b * ROWS + ahead * F, F), ROWS)

    def layer1(b):
        pre = mixed(lhs_f.at[0], a1h[inputs(b), :], a1l[inputs(b), :], False)
        pre = pre + jnp.concatenate([bcol[1]] * OUT, axis=0)
        a, d = silu_parts(pre)
        if b == 0:
            a, d = (without(x, 0, 1, me == 0) for x in (a, d))
        if b == NBLK - 1:
            a, d = (without(x, 5, 6, me == nchan - 1) for x in (a, d))
        a2h[outputs(b), :], a2l[outputs(b), :] = split(a)
        d1[outputs(b), :] = d

    run(NBLK, layer1)

    par = lax.rem(me, 2) * OWN

    def layer2(b):
        ah, al = a2h[inputs(b), :], a2l[inputs(b), :]
        pre = mixed(lhs_f.at[1], ah, al, False)
        pre = pre + jnp.concatenate([bcol[2]] * OUT, axis=0)
        a, d = silu_parts(pre)
        head = bcol[3]
        heads = hacc[...]
        grads = []
        for k in range(OUT):
            at = slice(k * F, k * F + F)
            row = jnp.sum(head * a[at], axis=0, keepdims=True)
            outs[pl.ds(par + OUT * b + k, 1), :] = row
            spot = pl.ds(OUT * b + k + HALO, 1)
            g_out = jnp.where(OUT * b + k < OWN, coef[spot, :], 0.0) * (row - sig[spot, :])
            heads = heads + g_out * a[at]
            grads.append((head * d[at]) * g_out)
        hacc[...] = heads
        g = jnp.concatenate(grads, axis=0)
        g2h[outputs(b, 2), :], g2l[outputs(b, 2), :] = split(g)
        add_channels(bacc.at[2], g)
        acc[1] += dot_t(shifted_triple(g), jnp.concatenate([ah, ah, al], axis=1))

    run(NBLK, layer2)

    outt[...] = outs[:128, :].T

    def back2(b):
        g_act = mixed(lhs_b.at[1], g2h[inputs(b), :], g2l[inputs(b), :], True)
        g = g_act * d1[outputs(b), :]
        g1h[outputs(b, 2), :], g1l[outputs(b, 2), :] = split(g)
        add_channels(bacc.at[1], g)
        ah, al = a1h[inputs(b), :], a1l[inputs(b), :]
        acc[0] += dot_t(shifted_triple(g), jnp.concatenate([ah, ah, al], axis=1))

    def push_out(k):
        peer = lax.rem(me + k, nchan)
        remote(outt.at[rows8(peer), :], got.at[rows8(me), :], 4, {"chan": peer}).start()

    run(NBLK, back2)

    ci = iota((F, COLS), 1) >> 5
    rows_of, pack_pw = {}, []
    for l in (1, 2):
        wide = jnp.concatenate([pw[l]] * INN, axis=1)
        grad_pw = jnp.zeros((F, COLS), F32)
        for tap in range(9):
            i, j = tap // 3, tap % 3
            total = jnp.zeros((F, COLS), F32)
            for co in range(OUT):
                at = slice(j * ROWS + co * F, j * ROWS + co * F + F)
                total = total + jnp.where(ci == co + i, acc[l - 1, at, :], 0.0)
            grad_pw = grad_pw + total * repeated(dw[l][tap])
            rows_of[l, tap] = fold(jnp.sum(total * wide, axis=0, keepdims=True))
        pack_pw.append(fold(grad_pw))
    pack_rows = [rows_of[l, tap] for tap in range(9) for l in (1, 2)]
    for sums in (bacc[1], bacc[2], hacc[...]):
        pack_rows.append(as_row(jnp.sum(sums, axis=1, keepdims=True))[:, :F])
    pack_rows.append(jnp.zeros((F - 21, F), F32))
    pack_pw.append(jnp.concatenate(pack_rows, axis=0))
    pack_pw.append(jnp.zeros((F, F), F32))
    pack[...] = jnp.concatenate(pack_pw, axis=1)

    def summed(ref, count):
        total = ref[0]
        for k in range(1, count):
            total = total + ref[k]
        return total

    near = 8
    far = nchan // near
    base = (me // near) * near

    def near_peer(k):
        return {"chan": base + lax.rem(me - base + k, near)}

    def far_peer(k):
        return {"chan": lax.rem(me + near * k, nchan)}

    def back1(b):
        g_act = mixed(lhs_b.at[0], g1h[inputs(b), :], g1l[inputs(b), :], True)
        g = g_act * d0[outputs(b), :]
        g0h[outputs(b), :], g0l[outputs(b), :] = split(g)
        add_channels(bacc.at[0], g)

    each(ntm, lambda k: remote(pack, ra.at[tm], 3, tm_peer(k)).start())
    ra[tm] = pack[...]
    run(NBLK + 1, back1)

    def grads0(b):
        parts = columns(b)
        hi = jnp.concatenate([p[0] for p in parts], axis=0)
        lo = jnp.concatenate([p[1] for p in parts], axis=0)
        at = pl.ds(aligned(b * 8 * F, F), 8 * F)
        gh, gl = g0h[at, :], g0l[at, :]
        left = jnp.concatenate([gh, gl, gh], axis=1)
        right = jnp.concatenate([hi, hi, lo], axis=1)
        acc0[...] += dot_t(left, right)

    run(9, grads0)

    lane48 = iota((F, 48), 1)
    firsts = []
    for tap in range(9):
        total = jnp.zeros((F, 48), F32)
        for co in range(8):
            here = lane48 == (tap % 3) * 16 + co + tap // 3
            total = total + jnp.where(here, acc0[co * F : co * F + F, :], 0.0)
        firsts.append(as_row(jnp.sum(total, axis=1, keepdims=True))[:, :128])
    firsts.append(as_row(jnp.sum(bacc[0], axis=1, keepdims=True))[:, :128])
    group = iota((1, 128), 1) >> 5
    for r in range(3):
        row = jnp.zeros((1, 128), F32)
        for q, first in enumerate(firsts[4 * r : 4 * r + 4]):
            row = jnp.where(group == q, first, row)
        pack0[r : r + 1, :] = row
    pack0[3:4, :] = jnp.zeros((1, 128), F32)
    each(ntm, lambda k: remote(pack0, r0a.at[tm], 7, tm_peer(k)).start())
    r0a[tm] = pack0[...]

    arrived(ra, ntm - 1, 3, tm_peer(1))
    va[...] = summed(ra, ntm)
    each(near, lambda k: remote(va, rb.at[me - base], 5, near_peer(k)).start())
    rb[me - base] = va[...]

    each(nchan, push_out)
    got[rows8(me), :] = outt[rows8(me), :]
    arrived(r0a, ntm - 1, 7, tm_peer(1))
    v0[...] = summed(r0a, ntm)
    each_chan(lambda k: remote(v0, r0b.at[me], 8, chan_peer(k)).start())
    r0b[me] = v0[...]

    arrived(rb, near - 1, 5, near_peer(1))
    vb[...] = summed(rb, near)
    each(far, lambda k: remote(vb, rc.at[me // near], 6, far_peer(k)).start())
    rc[me // near] = vb[...]

    arrived(got, 8 * (nchan - 1), 4, {"chan": right})
    lane = iota((8, 128), 1)
    for k in range(nchan // 2):
        den_out[:, 128 * k : 128 * k + 128] = jnp.where(
            lane < OWN, got[16 * k : 16 * k + 8, :], got[16 * k + 8 : 16 * k + 16, :]
        )
    arrived(r0b, nchan - 1, 8, {"chan": right})
    sums = summed(r0b, nchan)
    rows = [sums[k // 4 : k // 4 + 1, F * (k % 4) : F * (k % 4) + F] for k in range(10)]
    grad_pw = jnp.zeros((F, F), F32)
    final_rows = []
    for tap in range(9):
        column = as_column(rows[tap])
        grad_pw = grad_pw + column * dw[0][tap]
        final_rows.append(jnp.sum(column * pw[0], axis=0, keepdims=True))
    final_rows.append(rows[9])
    final_rows.append(jnp.zeros((1, F), F32))
    arrived(rc, far - 1, 6, far_peer(1))
    later_layers = summed(rc, far)
    all_rows = jnp.concatenate([later_layers[:21, 2 * F : 3 * F]] + final_rows, axis=0)
    total_out[...] = jnp.concatenate([later_layers[:, : 2 * F], all_rows, grad_pw], axis=1)


def unpack(den_ref, total_ref, dw_out, pw_out, bias_out, head_out, den_out):
    den_out[0] = den_ref[...]
    total = total_ref[...]
    pw_out[0] = total[:, 3 * F :]
    pw_out[1] = total[:, :F]
    pw_out[2] = total[:, F : 2 * F]
    rows = total[:, 2 * F : 3 * F]
    for tap in range(9):
        dw_out[tap, 0:1, :] = rows[21 + tap : 22 + tap]
        dw_out[tap, 1:3, :] = rows[2 * tap : 2 * tap + 2]
    bias_out[0:1, :] = rows[30:31]
    bias_out[1:3, :] = rows[18:20]
    head_out[...] = rows[20:21]


def vmem():
    return pl.BlockSpec(memory_space=pltpu.VMEM)


def on_device(ntm, nchan, recording, blind_mask, dw_kernels, pw_weights, biases, head_weights):
    sds = jax.ShapeDtypeStruct
    scale = SPOT_EVERY / (ntm * nchan * OWN * T)
    den, total = pl.pallas_call(
        functools.partial(step, ntm, nchan, scale),
        out_shape=(sds((8, OWN * nchan), F32), sds((F, 128), F32)),
        in_specs=[pl.BlockSpec(memory_space=pltpu.HBM)] * 6,
        out_specs=(vmem(),) * 2,
        scratch_shapes=[
            pltpu.VMEM((80, T), F32),
            pltpu.VMEM((80, T), F32),
            pltpu.VMEM((3, 80, T), F32),
            pltpu.VMEM((8 * F, 144), BF16),
            pltpu.VMEM((2, 3 * ROWS, 3 * COLS), BF16),
            pltpu.VMEM((2, 3 * ROWS, 3 * COLS), BF16),
            pltpu.VMEM((72 * F, T), BF16),
            pltpu.VMEM((72 * F, T), BF16),
            pltpu.VMEM((68 * F, T), BF16),
            pltpu.VMEM((68 * F, T), BF16),
            pltpu.VMEM((72 * F, T), F32),
            pltpu.VMEM((66 * F, T), F32),
            pltpu.VMEM((68 * F, T), BF16),
            pltpu.VMEM((68 * F, T), BF16),
            pltpu.VMEM((74 * F, T), BF16),
            pltpu.VMEM((74 * F, T), BF16),
            pltpu.VMEM((72 * F, T), BF16),
            pltpu.VMEM((72 * F, T), BF16),
            pltpu.VMEM((2, 3 * ROWS, COLS), F32),
            pltpu.VMEM((8 * F, 48), F32),
            pltpu.VMEM((3, F, T), F32),
            pltpu.VMEM((F, T), F32),
            pltpu.VMEM((4, F, T), F32),
            pltpu.VMEM((136, T), F32),
            pltpu.VMEM((1, 8, OWN * nchan), F32),
            pltpu.VMEM((9, 3, F), F32),
            pltpu.VMEM((3, F, F), F32),
            pltpu.VMEM((3, F), F32),
            pltpu.VMEM((1, F), F32),
            pltpu.SemaphoreType.DMA((6,)),
            pltpu.VMEM((T, 128), F32),
            pltpu.VMEM((T, 128), F32),
            pltpu.VMEM((96, T), jnp.int32),
            pltpu.VMEM((T, 128), F32),
            pltpu.VMEM((T, 128), F32),
            pltpu.VMEM((F, 128), F32),
            pltpu.VMEM((ntm, F, 128), F32),
            pltpu.VMEM((F, 128), F32),
            pltpu.VMEM((8, F, 128), F32),
            pltpu.VMEM((F, 128), F32),
            pltpu.VMEM((nchan // 8, F, 128), F32),
            pltpu.VMEM((4, 128), F32),
            pltpu.VMEM((ntm, 4, 128), F32),
            pltpu.VMEM((4, 128), F32),
            pltpu.VMEM((nchan, 4, 128), F32),
            pltpu.SemaphoreType.DMA((18,)),
        ],
        compiler_params=pltpu.CompilerParams(
            collective_id=0, has_side_effects=True, vmem_limit_bytes=62 << 20
        ),
        name="step",
    )(
        recording,
        blind_mask,
        jnp.transpose(dw_kernels, (2, 0, 1)),
        pw_weights,
        biases,
        head_weights.reshape(1, F),
    )
    dw_grad, pw_grad, bias_grad, head_grad, denoised = pl.pallas_call(
        unpack,
        out_shape=(
            sds((9, 3, F), F32),
            sds((3, F, F), F32),
            sds((3, F), F32),
            sds((1, F), F32),
            sds((1, 8, OWN * nchan), F32),
        ),
        in_specs=[vmem()] * 2,
        out_specs=(vmem(),) * 5,
        compiler_params=pltpu.CompilerParams(vmem_limit_bytes=62 << 20),
        name="unpack",
    )(den, total)
    return jnp.transpose(dw_grad, (1, 2, 0)), pw_grad, bias_grad, head_grad.reshape(F), denoised


def solution(mesh):
    placed = (P("tm", "chan", None), P("tm", "chan", None), P(), P(), P(), P())
    return jax.shard_map(
        functools.partial(on_device, mesh.shape["tm"], mesh.shape["chan"]),
        mesh=mesh,
        in_specs=placed,
        out_specs=(P(), P(), P(), P(), P("tm", "chan", None)),
        check_vma=False,
    )
```

```python
import functools

import jax
import jax.numpy as jnp
from jax import lax
from jax.experimental import pallas as pl
from jax.experimental.pallas import tpu as pltpu
from jax.sharding import PartitionSpec as P

SPOT_EVERY = 8
F = 32
T = 256
OWN = 64
HALO = 3
OUT = 6
INN = 8
ROWS = OUT * F
COLS = INN * F
NBLK = 11
MESH = pl.DeviceIdType.MESH
F32 = jnp.float32
BF16 = jnp.bfloat16


def aligned(start, size):
    return start if isinstance(start, int) else pl.multiple_of(start, size)


def run(count, body):
    for b in range(count):
        body(b)


def without(x, start, stop, outside):
    parts = [x[: start * F]] if start else []
    parts.append(jnp.where(outside, 0.0, x[start * F : stop * F]))
    if stop * F < x.shape[0]:
        parts.append(x[stop * F :])
    return jnp.concatenate(parts, axis=0)


def iota(shape, dim):
    return lax.broadcasted_iota(jnp.int32, shape, dim)


def split(x):
    hi = x.astype(BF16)
    return hi, (x - hi.astype(F32)).astype(BF16)


def later(x):
    first = iota((x.shape[0], 128), 1) == 0
    a, b = pltpu.roll(x[:, :128], 1, 1), pltpu.roll(x[:, 128:], 1, 1)
    return jnp.concatenate([jnp.where(first, 0.0, a), jnp.where(first, a, b)], axis=1)


def earlier(x):
    last = iota((x.shape[0], 128), 1) == 127
    a, b = pltpu.roll(x[:, :128], 127, 1), pltpu.roll(x[:, 128:], 127, 1)
    return jnp.concatenate([jnp.where(last, b, a), jnp.where(last, 0.0, b)], axis=1)


def dot(a, b):
    return jnp.dot(a, b, preferred_element_type=F32)


def dot_t(a, b):
    return lax.dot_general(a, b, (((1,), (1,)), ((), ())), preferred_element_type=F32)


def repeated(row):
    return jnp.concatenate([row] * INN, axis=1)


def as_column(row):
    return jnp.sum(jnp.where(iota((F, F), 0) == iota((F, F), 1), row, 0.0), axis=1, keepdims=True)


def as_row(column):
    same = iota((F, COLS), 0) == (iota((F, COLS), 1) & (F - 1))
    return jnp.sum(jnp.where(same, column, 0.0), axis=0, keepdims=True)


def fill_windows(rec_ref, send):
    lane = iota((8, 128), 1)
    tiles = rec_ref.shape[2] // 128
    zero = jnp.zeros((8, 128), F32)
    tile = [rec_ref[0, :, 128 * k : 128 * k + 128] for k in range(tiles)]
    for k in range(tiles):
        before = tile[k - 1] if k > 0 else zero
        after = tile[k + 1] if k < tiles - 1 else zero
        even = jnp.where(lane < HALO, pltpu.roll(before, HALO, 1), pltpu.roll(tile[k], HALO, 1))
        odd = jnp.where(
            lane < OWN + HALO,
            pltpu.roll(tile[k], OWN + HALO, 1),
            pltpu.roll(after, OWN + HALO, 1),
        )
        send[16 * k : 16 * k + 8, :] = even
        send[16 * k + 8 : 16 * k + 16, :] = odd


def forward_weights(lhs, pw, dw):
    wide = jnp.concatenate([pw] * INN, axis=1)
    ci = iota((F, COLS), 1) >> 5
    rows = [repeated(row) for row in dw]
    for j in range(3):
        for co in range(OUT):
            taps = jnp.zeros((F, COLS), F32)
            for i in range(3):
                taps = jnp.where(ci == co + i, rows[3 * i + j], taps)
            hi, lo = split(wide * taps)
            at = slice(j * ROWS + co * F, j * ROWS + co * F + F)
            lhs[at, 0:COLS] = hi
            lhs[at, COLS : 2 * COLS] = lo
            lhs[at, 2 * COLS : 3 * COLS] = hi


def backward_weights(lhs, pw_t, dw):
    wide = jnp.concatenate([pw_t] * INN, axis=1)
    ci = iota((F, COLS), 1) >> 5
    cols = [jnp.broadcast_to(as_column(row), (F, COLS)) for row in dw]
    for j in range(3):
        for co in range(OUT):
            taps = jnp.zeros((F, COLS), F32)
            for i in range(3):
                taps = jnp.where(ci == co + 2 - i, cols[3 * i + j], taps)
            hi, lo = split(wide * taps)
            at = slice(j * ROWS + co * F, j * ROWS + co * F + F)
            lhs[at, 0:COLS] = hi
            lhs[at, COLS : 2 * COLS] = lo
            lhs[at, 2 * COLS : 3 * COLS] = hi


def first_weights(lhs, pw, dw):
    lane = iota((F, 144), 1)
    part = (lane >= 48).astype(jnp.int32) + (lane >= 96).astype(jnp.int32)
    spot = lane - 48 * part
    j_of, ci = spot >> 4, spot & 15
    cols = [jnp.sum(pw * row, axis=1, keepdims=True) for row in dw]
    for co in range(8):
        taps = jnp.zeros((F, 144), F32)
        for tap in range(9):
            here = (ci == co + tap // 3) & (j_of == tap % 3)
            taps = jnp.where(here, cols[tap], taps)
        hi = taps.astype(BF16).astype(F32)
        lhs[co * F : co * F + F, :] = jnp.where(part == 1, taps - hi, hi).astype(BF16)


def tripled(hi, lo):
    return jnp.concatenate([hi, hi, lo], axis=0)


def silu_parts(pre):
    s = 0.5 * jnp.tanh(0.5 * pre) + 0.5
    a = pre * s
    return a, s + (a - a * s)


def mixed(lhs, hi, lo, flip):
    prod = dot(lhs[...], tripled(hi, lo))
    first, mid, last = prod[:ROWS], prod[ROWS : 2 * ROWS], prod[2 * ROWS :]
    if flip:
        first, last = last, first
    return mid + later(first) + earlier(last)


def fold(x):
    y = x[:, :128] + x[:, 128:]
    y = y + pltpu.roll(y, 64, 1)
    y = y + pltpu.roll(y, 32, 1)
    return y[:, :F]


def shifted_triple(g):
    hi, lo = split(g)
    parts = []
    for move in (earlier, lambda x: x, later):
        a, b = move(hi), move(lo)
        parts.append(jnp.concatenate([a, b, a], axis=1))
    return jnp.concatenate(parts, axis=0)


def add_channels(acc, g):
    total = acc[...]
    for k in range(OUT):
        total = total + g[k * F : k * F + F]
    acc[...] = total


def step(
    ntm, nchan, scale,
    rec_hbm, mask_hbm, dw_hbm, pw_hbm, bias_hbm, head_hbm, den_out, total_out,
    sig, coef, wins, lhs0, lhs_f, lhs_b, a1h, a1l, a2h, a2l, d0, d1,
    g2h, g2l, g1h, g1l, g0h, g0l, acc, acc0, bacc, hacc, bcol, outs,
    rec_ref, dw_ref, pw_ref, bias_ref, head_ref, lsems, send, win, maskx, outt, got,
    pack, ra, va, rb, vb, rc, pack0, r0a, v0, r0b, sems,
):
    me, tm = lax.axis_index("chan"), lax.axis_index("tm")
    right, left = lax.rem(me + 1, nchan), lax.rem(me + nchan - 1, nchan)
    barrier = pltpu.get_barrier_semaphore()

    def chan_peer(k):
        return {"chan": lax.rem(me + k, nchan)}

    def tm_peer(k):
        return {"tm": lax.rem(tm + k, ntm)}

    def each(count, go):
        def body(k, carry):
            go(k)
            return carry

        lax.fori_loop(1, count, body, 0)

    def each_chan(go):
        others = nchan - 8

        def body(k, carry):
            go(8 + lax.rem(k + 8, others))
            return carry

        lax.fori_loop(0, others, body, 0)
        each(8, go)

    def greet(where):
        pl.semaphore_signal(barrier, inc=1, device_id=where, device_id_type=MESH)

    def remote(src, dst, pair, where):
        return pltpu.make_async_remote_copy(
            src_ref=src,
            dst_ref=dst,
            send_sem=sems.at[2 * pair],
            recv_sem=sems.at[2 * pair + 1],
            device_id=where,
            device_id_type=MESH,
        )

    def rows8(index):
        return pl.ds(pl.multiple_of(index * 8, 8), 8)

    def arrived(dst, count, pair, where):
        remote(dst.at[pl.ds(0, count)], dst.at[pl.ds(0, count)], pair, where).wait()

    own_rows = pl.ds(8, OWN)
    loads = [
        pltpu.make_async_copy(src, dst, lsems.at[k])
        for k, (src, dst) in enumerate(
            (
                (rec_hbm, rec_ref),
                (mask_hbm.at[0], maskx.at[own_rows, :]),
                (dw_hbm, dw_ref),
                (pw_hbm, pw_ref),
                (bias_hbm, bias_ref),
                (head_hbm, head_ref),
            )
        )
    ]
    for load in loads:
        load.start()
    each_chan(lambda k: greet(chan_peer(k)))
    each(ntm, lambda k: greet(tm_peer(k)))
    loads[0].wait()
    fill_windows(rec_ref, send)
    for load in loads[1:]:
        load.wait()
    pl.semaphore_wait(barrier, nchan - 1 + ntm - 1)

    to_right = remote(
        maskx.at[pl.ds(OWN, 8), :], maskx.at[pl.ds(0, 8), :], 0, {"chan": right}
    )
    to_left = remote(
        maskx.at[pl.ds(8, 8), :], maskx.at[pl.ds(OWN + 8, 8), :], 1, {"chan": left}
    )

    def push_in(k):
        peer = lax.rem(me + k, nchan)
        remote(send.at[rows8(peer), :], win.at[rows8(me), :], 2, {"chan": peer}).start()

    each_chan(push_in)
    to_right.start()
    to_left.start()
    win[rows8(me), :] = send[rows8(me), :]
    maskx[OWN + 16 :, :] = jnp.zeros((16, T), jnp.int32)

    dw = [[dw_ref[tap, l : l + 1, :] for tap in range(9)] for l in range(3)]
    pw = [pw_ref[l] for l in range(3)]
    first_weights(lhs0, pw[0], dw[0])
    for l in (1, 2):
        forward_weights(lhs_f.at[l - 1], pw[l], dw[l])
        backward_weights(lhs_b.at[l - 1], pw[l].T, dw[l])
    for l in range(3):
        bcol[l] = jnp.broadcast_to(as_column(bias_ref[l : l + 1, :]), (F, T))
    bcol[3] = jnp.broadcast_to(as_column(head_ref[...]), (F, T))

    zero2 = jnp.zeros((2 * F, T), BF16)
    for ref in (g2h, g2l, g1h, g1l):
        ref[: 2 * F, :] = zero2
    for ref in (g1h, g1l):
        ref[68 * F :, :] = jnp.zeros((6 * F, T), BF16)
    for ref in (a2h, a2l):
        ref[66 * F :, :] = zero2
    acc0[...] = jnp.zeros_like(acc0)
    bacc[...] = jnp.zeros_like(bacc)
    hacc[...] = jnp.zeros_like(hacc)
    outs[...] = jnp.zeros_like(outs)

    to_right.wait()
    to_left.wait()
    arrived(win, 8 * (nchan - 1), 2, {"chan": right})
    turned = win[...].T
    sig[...] = turned[:80]
    blind = maskx[5:85, :] == 1
    coef[...] = jnp.where(blind, 2.0 * scale, 0.0)
    act0 = jnp.where(blind, 0.0, turned[:80])
    wins[0] = later(act0)
    wins[1] = act0
    wins[2] = earlier(act0)

    def columns(b):
        return [split(wins[j, pl.ds(aligned(8 * b, 8), 16), :]) for j in range(3)]

    def layer0(b):
        parts = columns(b)
        hi = jnp.concatenate([p[0] for p in parts], axis=0)
        lo = jnp.concatenate([p[1] for p in parts], axis=0)
        pre = dot(lhs0[...], tripled(hi, lo))
        pre = pre + jnp.concatenate([bcol[0]] * 8, axis=0)
        a, d = silu_parts(pre)
        if b == 0:
            a, d = (without(x, 0, 2, me == 0) for x in (a, d))
        if b == 8:
            a, d = (without(x, 2, 4, me == nchan - 1) for x in (a, d))
        at = pl.ds(aligned(b * 8 * F, F), 8 * F)
        a1h[at, :], a1l[at, :] = split(a)
        d0[at, :] = d

    run(9, layer0)

    def inputs(b):
        return pl.ds(aligned(b * ROWS, F), COLS)

    def outputs(b, ahead=0):
        return pl.ds(aligned(b * ROWS + ahead * F, F), ROWS)

    def layer1(b):
        pre = mixed(lhs_f.at[0], a1h[inputs(b), :], a1l[inputs(b), :], False)
        pre = pre + jnp.concatenate([bcol[1]] * OUT, axis=0)
        a, d = silu_parts(pre)
        if b == 0:
            a, d = (without(x, 0, 1, me == 0) for x in (a, d))
        if b == NBLK - 1:
            a, d = (without(x, 5, 6, me == nchan - 1) for x in (a, d))
        a2h[outputs(b), :], a2l[outputs(b), :] = split(a)
        d1[outputs(b), :] = d

    run(NBLK, layer1)

    par = lax.rem(me, 2) * OWN

    def layer2(b):
        ah, al = a2h[inputs(b), :], a2l[inputs(b), :]
        pre = mixed(lhs_f.at[1], ah, al, False)
        pre = pre + jnp.concatenate([bcol[2]] * OUT, axis=0)
        a, d = silu_parts(pre)
        head = bcol[3]
        heads = hacc[...]
        grads = []
        for k in range(OUT):
            at = slice(k * F, k * F + F)
            row = jnp.sum(head * a[at], axis=0, keepdims=True)
            outs[pl.ds(par + OUT * b + k, 1), :] = row
            spot = pl.ds(OUT * b + k + HALO, 1)
            g_out = jnp.where(OUT * b + k < OWN, coef[spot, :], 0.0) * (row - sig[spot, :])
            heads = heads + g_out * a[at]
            grads.append((head * d[at]) * g_out)
        hacc[...] = heads
        g = jnp.concatenate(grads, axis=0)
        g2h[outputs(b, 2), :], g2l[outputs(b, 2), :] = split(g)
        add_channels(bacc.at[2], g)
        part = dot_t(shifted_triple(g), jnp.concatenate([ah, ah, al], axis=1))
        acc[1] = part if b == 0 else acc[1] + part

    run(NBLK, layer2)

    outt[...] = outs[:128, :].T

    def back2(b):
        g_act = mixed(lhs_b.at[1], g2h[inputs(b), :], g2l[inputs(b), :], True)
        g = g_act * d1[outputs(b), :]
        g1h[outputs(b, 2), :], g1l[outputs(b, 2), :] = split(g)
        add_channels(bacc.at[1], g)
        ah, al = a1h[inputs(b), :], a1l[inputs(b), :]
        part = dot_t(shifted_triple(g), jnp.concatenate([ah, ah, al], axis=1))
        acc[0] = part if b == 0 else acc[0] + part

    def push_out(k):
        peer = lax.rem(me + k, nchan)
        remote(outt.at[rows8(peer), :], got.at[rows8(me), :], 4, {"chan": peer}).start()

    run(NBLK, back2)

    ci = iota((F, COLS), 1) >> 5
    rows_of, pack_pw = {}, []
    for l in (1, 2):
        wide = jnp.concatenate([pw[l]] * INN, axis=1)
        grad_pw = jnp.zeros((F, COLS), F32)
        for tap in range(9):
            i, j = tap // 3, tap % 3
            total = jnp.zeros((F, COLS), F32)
            for co in range(OUT):
                at = slice(j * ROWS + co * F, j * ROWS + co * F + F)
                total = total + jnp.where(ci == co + i, acc[l - 1, at, :], 0.0)
            grad_pw = grad_pw + total * repeated(dw[l][tap])
            rows_of[l, tap] = fold(jnp.sum(total * wide, axis=0, keepdims=True))
        pack_pw.append(fold(grad_pw))
    pack_rows = [rows_of[l, tap] for tap in range(9) for l in (1, 2)]
    for sums in (bacc[1], bacc[2], hacc[...]):
        pack_rows.append(as_row(jnp.sum(sums, axis=1, keepdims=True))[:, :F])
    pack_rows.append(jnp.zeros((F - 21, F), F32))
    pack_pw.append(jnp.concatenate(pack_rows, axis=0))
    pack_pw.append(jnp.zeros((F, F), F32))
    pack[...] = jnp.concatenate(pack_pw, axis=1)

    def summed(ref, count):
        total = ref[0]
        for k in range(1, count):
            total = total + ref[k]
        return total

    near = 8
    far = nchan // near
    base = (me // near) * near

    def near_peer(k):
        return {"chan": base + lax.rem(me - base + k, near)}

    def far_peer(k):
        return {"chan": lax.rem(me + near * k, nchan)}

    def back1(b):
        g_act = mixed(lhs_b.at[0], g1h[inputs(b), :], g1l[inputs(b), :], True)
        g = g_act * d0[outputs(b), :]
        g0h[outputs(b), :], g0l[outputs(b), :] = split(g)
        add_channels(bacc.at[0], g)

    each(ntm, lambda k: remote(pack, ra.at[tm], 3, tm_peer(k)).start())
    ra[tm] = pack[...]
    run(NBLK + 1, back1)

    def grads0(b):
        parts = columns(b)
        hi = jnp.concatenate([p[0] for p in parts], axis=0)
        lo = jnp.concatenate([p[1] for p in parts], axis=0)
        at = pl.ds(aligned(b * 8 * F, F), 8 * F)
        gh, gl = g0h[at, :], g0l[at, :]
        left = jnp.concatenate([gh, gl, gh], axis=1)
        right = jnp.concatenate([hi, hi, lo], axis=1)
        acc0[...] += dot_t(left, right)

    run(9, grads0)

    lane48 = iota((F, 48), 1)
    firsts = []
    for tap in range(9):
        total = jnp.zeros((F, 48), F32)
        for co in range(8):
            here = lane48 == (tap % 3) * 16 + co + tap // 3
            total = total + jnp.where(here, acc0[co * F : co * F + F, :], 0.0)
        firsts.append(as_row(jnp.sum(total, axis=1, keepdims=True))[:, :128])
    firsts.append(as_row(jnp.sum(bacc[0], axis=1, keepdims=True))[:, :128])
    group = iota((1, 128), 1) >> 5
    for r in range(3):
        row = jnp.zeros((1, 128), F32)
        for q, first in enumerate(firsts[4 * r : 4 * r + 4]):
            row = jnp.where(group == q, first, row)
        pack0[r : r + 1, :] = row
    each(ntm, lambda k: remote(pack0, r0a.at[tm], 7, tm_peer(k)).start())
    r0a[tm] = pack0[...]

    arrived(ra, ntm - 1, 3, tm_peer(1))
    va[...] = summed(ra, ntm)
    each(near, lambda k: remote(va, rb.at[me - base], 5, near_peer(k)).start())
    rb[me - base] = va[...]

    each(nchan, push_out)
    got[rows8(me), :] = outt[rows8(me), :]
    arrived(r0a, ntm - 1, 7, tm_peer(1))
    v0[...] = summed(r0a, ntm)
    each_chan(lambda k: remote(v0, r0b.at[me], 8, chan_peer(k)).start())
    r0b[me] = v0[...]

    arrived(rb, near - 1, 5, near_peer(1))
    vb[...] = summed(rb, near)
    each(far, lambda k: remote(vb, rc.at[me // near], 6, far_peer(k)).start())
    rc[me // near] = vb[...]

    arrived(got, 8 * (nchan - 1), 4, {"chan": right})
    lane = iota((8, 128), 1)
    for k in range(nchan // 2):
        den_out[:, 128 * k : 128 * k + 128] = jnp.where(
            lane < OWN, got[16 * k : 16 * k + 8, :], got[16 * k + 8 : 16 * k + 16, :]
        )
    arrived(r0b, nchan - 1, 8, {"chan": right})
    sums = summed(r0b, nchan)
    rows = [sums[k // 4 : k // 4 + 1, F * (k % 4) : F * (k % 4) + F] for k in range(10)]
    grad_pw = jnp.zeros((F, F), F32)
    final_rows = []
    for tap in range(9):
        column = as_column(rows[tap])
        grad_pw = grad_pw + column * dw[0][tap]
        final_rows.append(jnp.sum(column * pw[0], axis=0, keepdims=True))
    final_rows.append(rows[9])
    final_rows.append(jnp.zeros((1, F), F32))
    arrived(rc, far - 1, 6, far_peer(1))
    later_layers = summed(rc, far)
    all_rows = jnp.concatenate([later_layers[:21, 2 * F : 3 * F]] + final_rows, axis=0)
    total_out[...] = jnp.concatenate([later_layers[:, : 2 * F], all_rows, grad_pw], axis=1)


def unpack(den_ref, total_ref, dw_out, pw_out, bias_out, head_out, den_out):
    den_out[0] = den_ref[...]
    total = total_ref[...]
    pw_out[0] = total[:, 3 * F :]
    pw_out[1] = total[:, :F]
    pw_out[2] = total[:, F : 2 * F]
    rows = total[:, 2 * F : 3 * F]
    for tap in range(9):
        dw_out[tap, 0:1, :] = rows[21 + tap : 22 + tap]
        dw_out[tap, 1:3, :] = rows[2 * tap : 2 * tap + 2]
    bias_out[0:1, :] = rows[30:31]
    bias_out[1:3, :] = rows[18:20]
    head_out[...] = rows[20:21]


def vmem():
    return pl.BlockSpec(memory_space=pltpu.VMEM)


def on_device(ntm, nchan, recording, blind_mask, dw_kernels, pw_weights, biases, head_weights):
    sds = jax.ShapeDtypeStruct
    scale = SPOT_EVERY / (ntm * nchan * OWN * T)
    den, total = pl.pallas_call(
        functools.partial(step, ntm, nchan, scale),
        out_shape=(sds((8, OWN * nchan), F32), sds((F, 128), F32)),
        in_specs=[pl.BlockSpec(memory_space=pltpu.HBM)] * 6,
        out_specs=(vmem(),) * 2,
        scratch_shapes=[
            pltpu.VMEM((80, T), F32),
            pltpu.VMEM((80, T), F32),
            pltpu.VMEM((3, 80, T), F32),
            pltpu.VMEM((8 * F, 144), BF16),
            pltpu.VMEM((2, 3 * ROWS, 3 * COLS), BF16),
            pltpu.VMEM((2, 3 * ROWS, 3 * COLS), BF16),
            pltpu.VMEM((72 * F, T), BF16),
            pltpu.VMEM((72 * F, T), BF16),
            pltpu.VMEM((68 * F, T), BF16),
            pltpu.VMEM((68 * F, T), BF16),
            pltpu.VMEM((72 * F, T), F32),
            pltpu.VMEM((66 * F, T), F32),
            pltpu.VMEM((68 * F, T), BF16),
            pltpu.VMEM((68 * F, T), BF16),
            pltpu.VMEM((74 * F, T), BF16),
            pltpu.VMEM((74 * F, T), BF16),
            pltpu.VMEM((72 * F, T), BF16),
            pltpu.VMEM((72 * F, T), BF16),
            pltpu.VMEM((2, 3 * ROWS, COLS), F32),
            pltpu.VMEM((8 * F, 48), F32),
            pltpu.VMEM((3, F, T), F32),
            pltpu.VMEM((F, T), F32),
            pltpu.VMEM((4, F, T), F32),
            pltpu.VMEM((136, T), F32),
            pltpu.VMEM((1, 8, OWN * nchan), F32),
            pltpu.VMEM((9, 3, F), F32),
            pltpu.VMEM((3, F, F), F32),
            pltpu.VMEM((3, F), F32),
            pltpu.VMEM((1, F), F32),
            pltpu.SemaphoreType.DMA((6,)),
            pltpu.VMEM((T, 128), F32),
            pltpu.VMEM((T, 128), F32),
            pltpu.VMEM((96, T), jnp.int32),
            pltpu.VMEM((T, 128), F32),
            pltpu.VMEM((T, 128), F32),
            pltpu.VMEM((F, 128), F32),
            pltpu.VMEM((ntm, F, 128), F32),
            pltpu.VMEM((F, 128), F32),
            pltpu.VMEM((8, F, 128), F32),
            pltpu.VMEM((F, 128), F32),
            pltpu.VMEM((nchan // 8, F, 128), F32),
            pltpu.VMEM((3, 128), F32),
            pltpu.VMEM((ntm, 3, 128), F32),
            pltpu.VMEM((3, 128), F32),
            pltpu.VMEM((nchan, 3, 128), F32),
            pltpu.SemaphoreType.DMA((18,)),
        ],
        compiler_params=pltpu.CompilerParams(
            collective_id=0, has_side_effects=True, vmem_limit_bytes=62 << 20
        ),
        name="step",
    )(
        recording,
        blind_mask,
        jnp.transpose(dw_kernels, (2, 0, 1)),
        pw_weights,
        biases,
        head_weights.reshape(1, F),
    )
    dw_grad, pw_grad, bias_grad, head_grad, denoised = pl.pallas_call(
        unpack,
        out_shape=(
            sds((9, 3, F), F32),
            sds((3, F, F), F32),
            sds((3, F), F32),
            sds((1, F), F32),
            sds((1, 8, OWN * nchan), F32),
        ),
        in_specs=[vmem()] * 2,
        out_specs=(vmem(),) * 5,
        compiler_params=pltpu.CompilerParams(vmem_limit_bytes=62 << 20),
        name="unpack",
    )(den, total)
    return jnp.transpose(dw_grad, (1, 2, 0)), pw_grad, bias_grad, head_grad.reshape(F), denoised


def solution(mesh):
    placed = (P("tm", "chan", None), P("tm", "chan", None), P(), P(), P(), P())
    return jax.shard_map(
        functools.partial(on_device, mesh.shape["tm"], mesh.shape["chan"]),
        mesh=mesh,
        in_specs=placed,
        out_specs=(P(), P(), P(), P(), P("tm", "chan", None)),
        check_vma=False,
    )
```
